32 devices in a mesh: grp: 2 (over x), seq: 16 (over z, y, core).
Axes of the slice: x: 2, y: 2, z: 4, core: 2. Of those that a mesh axis runs over, the one named last changes fastest.
Arguments:
- query_inputs: bfloat16 [32768, 128], P(('grp', 'seq')), parts along dimension 0, may hold values from -6 to 6
- key_inputs: bfloat16 [32768, 128], P(('grp', 'seq')), parts along dimension 0, may hold values from -5.3 to 4.8
- value_inputs: bfloat16 [32768, 2048], P(('grp', 'seq')), parts along dimension 0, may hold values from -5.3 to 4.8
- log_decay: float32 [16, 32768], P(None, ('grp', 'seq')), parts along dimension 1, may hold values from -0.9 to 0, as said below
- level_weight: bfloat16 [15, 16, 32768], P(None, None, ('grp', 'seq')), parts along dimension 2, may hold values from 0.099609375 to 1
- conv_weight: float32 [4, 2304], replicated, may hold values from 0.35 to 0.65
- norm_gain: float32 [2048], replicated, may hold values from 0.1 to 1.9
Outputs:
- mixer_out: bfloat16 [32768, 2048], P(('grp', 'seq')), parts along dimension 0
The draws below stay inside these ranges and needn't reach their ends.
There are 2 independent parts, one for each index of `grp`. The reference program is written for one: setup_inputs(seed, part) draws one part's arguments, and reference() takes and returns one part's arrays. A program takes and returns all parts, laid end to end along the dimension named above; an argument that names none is the same for every part. Nothing has to cross between parts.
Inputs may be any that keep to these rules, and one draw needn't show every extreme that they name: `log_decay`: each entry is the logarithm of one head's decay factor at one token.
All inputs are finite; a program needn't handle non-finite values.
Results may differ from the reference program's by a relative error of at most 0.014.
Values may be sent and summed in bfloat16 or wider, within the bound.
No kernel may reach another device: no remote copies, remote signals or barrier semaphores. Data moves between devices by JAX's collectives and lax.ppermute only.
A program may use at most 64 MiB of HBM per device.

```python
import math
import jax
import jax.numpy as jnp
import numpy as np
from jax import lax

HEAD_TOTAL = 16
HEAD_DIM = 128
STATE = 128
KERNEL = 4
TOK_DEV = 1024
LOG_TOK = 10
LOG_SEQ = 4
LEVELS = 15
TOKEN_TOTAL = 16384
N_SEQ = 16


def draw_log_decay(key, part):
    random_subkeys = jax.random.split(key, 8)
    keep_share = 0.5
    middle_share = 0.25
    shard_count = TOKEN_TOTAL // TOK_DEV
    shard_ordinal = jax.random.permutation(random_subkeys[0], HEAD_TOTAL).astype(jnp.float32)
    keeper = shard_ordinal < HEAD_TOTAL * keep_share
    middle = jnp.logical_and(jnp.logical_not(keeper), shard_ordinal < HEAD_TOTAL * (keep_share + middle_share))
    quick_decay_heads = jnp.logical_and(jnp.logical_not(keeper), jnp.logical_not(middle))
    fast_rate = jnp.exp(jax.random.uniform(random_subkeys[1], (HEAD_TOTAL,), jnp.float32, math.log(0.06), math.log(0.15)))
    keep_rate = jnp.exp(jax.random.uniform(random_subkeys[2], (HEAD_TOTAL,), jnp.float32, math.log(0.15 / TOKEN_TOTAL), math.log(0.75 / TOKEN_TOTAL)))
    middle_rate = jnp.exp(jax.random.uniform(random_subkeys[7], (HEAD_TOTAL,), jnp.float32, math.log(0.15 / TOK_DEV), math.log(1.5 / TOK_DEV)))
    head_decay_rate = jnp.where(keeper, keep_rate, jnp.where(middle, middle_rate, fast_rate))
    shard_factor = jnp.exp(jax.random.uniform(random_subkeys[3], (HEAD_TOTAL, shard_count, 1), jnp.float32, -0.7, 0.7))
    token_factor = jnp.exp(jax.random.uniform(random_subkeys[4], (HEAD_TOTAL, shard_count, TOK_DEV), jnp.float32, -0.7, 0.7))
    growth_multiplier = (shard_factor * token_factor).reshape(HEAD_TOTAL, TOKEN_TOTAL)
    span_start_positions = jax.random.randint(random_subkeys[5], (2, HEAD_TOTAL), 0, TOKEN_TOTAL)
    sampled_span_lengths = jnp.log(1.0 - jax.random.uniform(random_subkeys[6], (2, HEAD_TOTAL), jnp.float32, 0.2, 0.5))
    leading_row = jnp.where(shard_ordinal == 0.0, math.log(0.4), sampled_span_lengths[0])
    span_lengths = jnp.stack([leading_row, sampled_span_lengths[1]], axis=0)
    position_list = jnp.arange(TOKEN_TOTAL, dtype=jnp.int32)
    token_spans = jnp.zeros((HEAD_TOTAL, TOKEN_TOTAL), jnp.float32)
    for span_position in range(2):
        token_spans = token_spans + jnp.where(position_list[None, :] == span_start_positions[span_position][:, None], span_lengths[span_position][:, None], 0.0)
    token_spans = jnp.where(quick_decay_heads[:, None], 0.0, token_spans)
    return jnp.maximum(-(head_decay_rate[:, None] * growth_multiplier) + token_spans, -0.9)


def centred_inputs(key, column_count):
    random_part = jnp.clip(jax.random.normal(key, (TOKEN_TOTAL, column_count), jnp.float32), -5.0, 5.0)
    return (random_part - 0.255).astype(jnp.bfloat16)


def draw_key_inputs(key, part):
    return centred_inputs(jax.random.fold_in(key, 17), STATE)


def draw_value_inputs(key, part):
    return centred_inputs(jax.random.fold_in(key, 29), HEAD_TOTAL * HEAD_DIM)


def draw_conv_weight(key, part):
    return jax.random.uniform(jax.random.fold_in(key, 41), (KERNEL, 2 * STATE + HEAD_TOTAL * HEAD_DIM), jnp.float32, 0.35, 0.65)


def block_levels(key, dims, cuts, least, top_value):
    loudness, own = 1.0, jax.random.fold_in(key, 6)
    for axis_at, blocks in cuts:
        heights = jnp.exp(jax.random.uniform(jax.random.fold_in(own, axis_at), (blocks,), jnp.float32, least / len(cuts), top_value / len(cuts)))
        loudness = loudness * jnp.repeat(heights, dims[axis_at] // blocks).reshape([-1 if axis == axis_at else 1 for axis in range(len(dims))])
    return loudness


def centred(own_key, extent, spread, reach, cuts=(), kind=jnp.bfloat16):
    level = block_levels(own_key, extent, cuts, -0.22, 0.18) if cuts else 1.0
    drawn = jax.random.normal(own_key, extent, jnp.float32) * spread * level
    return jnp.minimum(jnp.maximum(drawn, -reach), reach).astype(kind)


def setup_inputs(seed: int = 0, part: int = 0) -> dict:
    seeds = jax.random.split(jax.random.key(seed), 8)
    part_keys = jax.random.split(jax.random.fold_in(seeds[7], part), 8)
    query_inputs = centred(part_keys[0], (TOKEN_TOTAL, STATE), 1.0, 6.0, ((0, 16),))
    key_inputs = draw_key_inputs(jax.random.fold_in(jax.random.fold_in(seeds[7], part), 71), part)
    value_inputs = draw_value_inputs(jax.random.fold_in(jax.random.fold_in(seeds[7], part), 71), part)
    log_decay = draw_log_decay(jax.random.fold_in(jax.random.fold_in(seeds[7], part), 71), part)
    level_weight = jnp.clip(jnp.exp(math.log(1.0) - 2.306499 * jax.random.uniform(part_keys[4], (LEVELS, HEAD_TOTAL, TOKEN_TOTAL), jnp.float32) ** block_levels(part_keys[4], (LEVELS, HEAD_TOTAL, TOKEN_TOTAL), ((2, 16),), -0.2, 0.2)), 0.099609375, 1.0).astype(jnp.bfloat16)
    conv_weight = draw_conv_weight(jax.random.fold_in(seeds[7], 71), part)
    norm_gain = jnp.clip(1.0 + 0.18 * jax.random.normal(seeds[6], (HEAD_TOTAL * HEAD_DIM,), jnp.float32), 0.1, 1.9)
    return {"query_inputs": query_inputs, "key_inputs": key_inputs, "value_inputs": value_inputs, "log_decay": log_decay, "level_weight": level_weight, "conv_weight": conv_weight, "norm_gain": norm_gain}


EPSILON = 1e-05

def causal_conv(inputs, weight):
    tap_count = weight.shape[0]
    length = inputs.shape[0]
    padded = jnp.concatenate([jnp.zeros((tap_count - 1, inputs.shape[1]), inputs.dtype), inputs], axis=0).astype(jnp.float32)
    summed = jnp.zeros(inputs.shape, jnp.float32)
    for tap_pos in range(tap_count):
        summed = summed + weight[tap_pos][None, :] * padded[tap_pos:tap_pos + length]
    return jax.nn.silu(summed).astype(jnp.bfloat16)

def reference(query_inputs, key_inputs, value_inputs, log_decay, level_weight, conv_weight, norm_gain):
    queries = causal_conv(query_inputs, conv_weight[:, :STATE])
    keys_conv = causal_conv(key_inputs, conv_weight[:, STATE:2 * STATE])
    values_conv = causal_conv(value_inputs, conv_weight[:, 2 * STATE:])
    cumul_decay = jnp.cumsum(log_decay.reshape(HEAD_TOTAL, N_SEQ, TOK_DEV), axis=2)
    cumul_shards = jnp.transpose(cumul_decay, (1, 0, 2))
    query_shards = queries.reshape(N_SEQ, TOK_DEV, STATE)
    key_shards = keys_conv.reshape(N_SEQ, TOK_DEV, STATE)
    value_shards = values_conv.reshape(N_SEQ, TOK_DEV, HEAD_TOTAL, HEAD_DIM)
    weight_shards = jnp.transpose(level_weight.reshape(LEVELS, HEAD_TOTAL, N_SEQ, TOK_DEV), (2, 0, 1, 3))

    def group_of(inputs):
        key_rows, value_rows, cumul_rows = inputs
        tail_decay = jnp.exp(cumul_rows[:, TOK_DEV - 1:] - cumul_rows)
        decayed = (key_rows.astype(jnp.float32)[None, :, :] * tail_decay[:, :, None]).astype(jnp.bfloat16)
        return jnp.einsum('hcn,chp->hnp', decayed.astype(jnp.float32), value_rows.astype(jnp.float32))
    group_state = lax.map(group_of, (key_shards, value_shards, cumul_shards))
    shard_ids = np.arange(N_SEQ)
    block_state = group_state
    block_total = cumul_shards[:, :, TOK_DEV - 1]
    offset = jnp.zeros_like(block_total)
    buckets = []
    for bit_pos in range(LOG_SEQ):
        partner = jnp.asarray((shard_ids ^ 1 << bit_pos).astype(np.int32))
        other_state = block_state[partner]
        other_total = block_total[partner]
        upper_half = shard_ids >> bit_pos & 1 == 1
        upper_state = upper_half[:, None, None, None]
        lifted = jnp.exp(offset)[:, :, None, None] * other_state
        buckets.append(jnp.where(upper_state, lifted, 0.0).astype(jnp.bfloat16))
        block_state = jnp.where(upper_state, block_state + jnp.exp(block_total)[:, :, None, None] * other_state, other_state + jnp.exp(other_total)[:, :, None, None] * block_state)
        block_total = block_total + other_total
        offset = offset + jnp.where(upper_half[:, None], other_total, 0.0)
    bucket_all = jnp.stack(buckets, axis=1)

    def shard_out(inputs):
        query_rows, key_rows, value_rows, cumul_rows, weight_rows, bucket_rows = inputs
        scores = jnp.dot(query_rows, key_rows.T, preferred_element_type=jnp.float32)
        position_list = jnp.arange(TOK_DEV, dtype=jnp.int32)
        differ = jnp.bitwise_xor(position_list[:, None], position_list[None, :])
        levels = jnp.zeros((TOK_DEV, TOK_DEV), jnp.int32)
        for bit_pos in range(LOG_TOK):
            levels = levels + (differ >= 1 << bit_pos).astype(jnp.int32)
        causal = position_list[:, None] >= position_list[None, :]
        query_float = query_rows.astype(jnp.float32)

        def head_out(head_idx):
            decay_row = cumul_rows[head_idx]
            weights_row = weight_rows[:, head_idx].astype(jnp.float32)
            mixing = jnp.zeros((TOK_DEV, TOK_DEV), jnp.float32)
            for level_pos in range(LOG_TOK + 1):
                mixing = mixing + jnp.where(levels == level_pos, weights_row[level_pos][:, None], 0.0)
            decay_gap = jnp.where(causal, decay_row[:, None] - decay_row[None, :], -1e+30)
            near_weight = (scores * mixing * jnp.exp(decay_gap)).astype(jnp.bfloat16)
            near_term = jnp.dot(near_weight, value_rows[:, head_idx], preferred_element_type=jnp.float32)
            far_scale = weights_row[LOG_TOK + 1:] * jnp.exp(decay_row)[None, :]
            far_query = (query_float[:, None, :] * far_scale.T[:, :, None]).astype(jnp.bfloat16).reshape(TOK_DEV, LOG_SEQ * STATE)
            head_buckets = bucket_rows[:, head_idx].reshape(LOG_SEQ * STATE, HEAD_DIM)
            pre_norm = near_term + jnp.dot(far_query, head_buckets, preferred_element_type=jnp.float32)
            gain_row = lax.dynamic_slice_in_dim(norm_gain, head_idx * HEAD_DIM, HEAD_DIM)
            normed = pre_norm * lax.rsqrt(lax.optimization_barrier(jnp.mean(pre_norm * pre_norm, axis=1, keepdims=True)) + EPSILON) * gain_row[None, :]
            return normed.astype(jnp.bfloat16)
        per_head = lax.map(head_out, jnp.arange(HEAD_TOTAL, dtype=jnp.int32))
        return jnp.transpose(per_head, (1, 0, 2)).reshape(TOK_DEV, HEAD_TOTAL * HEAD_DIM)
    shard_outputs = lax.map(shard_out, (query_shards, key_shards, value_shards, cumul_shards, weight_shards, bucket_all))
    return shard_outputs.reshape(TOKEN_TOTAL, HEAD_TOTAL * HEAD_DIM)
```

```python
import functools

import jax
import jax.numpy as jnp
from jax import lax
from jax.experimental import pallas as pl
from jax.experimental.pallas import tpu as pltpu
from jax.sharding import PartitionSpec as P


EPSILON = 1e-05
TILE = 128
GROUP = 16
NEAR_CALLS = 2
STEP = 2
NEVER = -1e30


def log2(value):
    return value.bit_length() - 1


def whole(array):
    rank = array.ndim
    return pl.BlockSpec(array.shape, lambda i: (0,) * rank)


def shape_of(shape, dtype):
    return jax.ShapeDtypeStruct(shape, dtype)


def tile_decays(log_decay):
    length = log_decay.shape[1]
    row = lax.broadcasted_iota(jnp.int32, (TILE, TILE), 0)
    col = lax.broadcasted_iota(jnp.int32, (TILE, TILE), 1)
    parts = [log_decay[:, at : at + TILE] for at in range(0, length, TILE)]
    local = lax.dot_general(
        jnp.concatenate(parts, axis=0),
        (row <= col).astype(jnp.float32),
        (((1,), (0,)), ((), ())),
        precision=lax.Precision.HIGHEST,
        preferred_element_type=jnp.float32,
    )
    middle = jnp.broadcast_to(local[:, TILE // 2 - 1 : TILE // 2], local.shape)
    total = jnp.broadcast_to(local[:, TILE - 1 : TILE], local.shape)
    heads = log_decay.shape[0]

    def split(array):
        return [array[at : at + heads] for at in range(0, array.shape[0], heads)]

    return split(local), split(middle), split(total)


def pair_row(table, head, pair):
    sides = [table[2 * pair + side, pl.ds(head, 1), :] for side in range(2)]
    return jnp.concatenate(sides, axis=1)


def conv_tile(buf, weight, start):
    taps = weight.shape[0]
    total = None
    for tap in range(taps):
        term = weight[tap : tap + 1, :] * buf[pl.ds(8 - (taps - 1) + tap + start, TILE), :]
        total = term if total is None else total + term
    return total + total * jnp.tanh(total)


def fill(buf, source, rim):
    length = source.shape[0]
    buf[pl.ds(8 - rim.shape[0], rim.shape[0]), :] = rim[...].astype(jnp.float32)
    buf[pl.ds(8, length), :] = source[...].astype(jnp.float32)


def state_keys(pairs):
    return [
        (bit, first)
        for bit in range(log2(pairs))
        for first in range(0, pairs, 2 << bit)
    ]


def three_terms(wide):
    terms = []
    for _ in range(3):
        term = wide.astype(jnp.bfloat16)
        terms.append(term)
        wide = wide - term.astype(jnp.float32)
    terms.append(jnp.zeros_like(terms[0]))
    return jnp.concatenate(terms, axis=0)


def sum_terms(terms):
    each = terms.shape[0] // 4
    wide = terms.astype(jnp.float32)
    return wide[:each] + wide[each : 2 * each] + wide[2 * each : 3 * each]


def state_kernel(
    q_ref, k_ref, v_ref, rq_ref, rk_ref, rv_ref, wq_ref, wk_ref, wv_ref, ld_ref,
    vt_ref, st_ref, g_ref, qt_ref, kc_ref,
    buf, scale, total,
):
    step = pl.program_id(0)
    heads = ld_ref.shape[0]
    length = v_ref.shape[0]
    width = v_ref.shape[1] // STEP
    pairs = length // (2 * TILE)

    @pl.when(step == 0)
    def _():
        local, _, totals = tile_decays(ld_ref[...])
        summed = None
        for pair in range(pairs):
            low, high = 2 * pair, 2 * pair + 1
            scale[low] = jnp.exp(totals[low] - local[low] + totals[high])
            scale[high] = jnp.exp(totals[high] - local[high])
            both = totals[low] + totals[high]
            total[pair] = jnp.exp(both)
            summed = both if summed is None else summed + both
        g_ref[pl.ds(heads * width, 4 * heads), :] = three_terms(summed)
        fill(buf.at[0], q_ref, rq_ref)
        fill(buf.at[1], k_ref, rk_ref)
        for tile in range(length // TILE):
            at = tile * TILE
            done = conv_tile(buf.at[0], 0.5 * wq_ref[...], at).astype(jnp.bfloat16)
            qt_ref[:, at : at + TILE] = done.T
            kc_ref[at : at + TILE, :] = conv_tile(buf.at[1], 0.5 * wk_ref[...], at).astype(jnp.bfloat16)

    for place in range(STEP):
        lanes = slice(place * width, (place + 1) * width)
        fill(buf.at[place], v_ref.at[:, lanes], rv_ref.at[:, lanes])
    for place in range(STEP):
        head = step * STEP + place
        lanes = slice(place * width, (place + 1) * width)
        weight = 0.5 * wv_ref[:, lanes]
        states = {}
        for pair in range(pairs):
            at = 2 * pair * TILE
            sides = []
            for start in (at, at + TILE):
                done = conv_tile(buf.at[place], weight, start).astype(jnp.bfloat16).T
                vt_ref[lanes, start : start + TILE] = done
                sides.append(done)
            row = pair_row(scale, head, pair).astype(jnp.bfloat16)
            states[(0, pair)] = jnp.dot(
                jnp.concatenate(sides, axis=1) * row,
                kc_ref[at : at + 2 * TILE, :],
                preferred_element_type=jnp.float32,
            )
        decay = [total[pair, pl.ds(head, 1), :] for pair in range(pairs)]
        for bit in range(log2(pairs)):
            for first in range(0, pairs, 2 << bit):
                keep = states[(bit, first + (1 << bit))]
                factor = decay[first + (1 << bit)]
                for later in range(first + (1 << bit) + 1, first + (2 << bit)):
                    factor = factor * decay[later]
                states[(bit + 1, first)] = keep + factor * states[(bit, first)]
        for order, key in enumerate(state_keys(pairs)):
            st_ref[order, lanes, :] = states[key].astype(jnp.bfloat16)
        at = pl.multiple_of(head * width, width)
        g_ref[pl.ds(at, width), :] = states[(log2(pairs), 0)].astype(jnp.bfloat16)


def table_rows(length):
    inner = log2(GROUP) + 1
    groups = TILE // GROUP
    states = log2(length // (2 * TILE))
    return {
        "inner": 0,
        "group": inner,
        "sibling": inner + groups,
        "value": inner + groups + 1,
        "state": inner + groups + 2,
        "size": inner + groups + 2 + states,
    }


def table_kernel(ld_ref, lw_ref, tab_ref, far_ref):
    heads, length = ld_ref.shape
    levels = lw_ref.shape[0]
    pairs = length // (2 * TILE)
    rows = table_rows(length)
    inner = log2(GROUP) + 1
    tile_level = log2(TILE)
    locals_, middles, totals = tile_decays(ld_ref[...])
    block = lax.broadcasted_iota(jnp.int32, (heads, TILE), 1) // GROUP
    zero = jnp.zeros((heads, TILE), jnp.float32)
    pair_total = []
    running = zero
    for pair in range(pairs):
        low = 2 * pair
        for tile in (low, low + 1):
            lanes = pl.ds(tile * TILE, TILE)
            weight = [lw_ref[level, :, lanes].astype(jnp.float32) for level in range(levels)]
            local = locals_[tile]
            gap = jnp.exp(local - middles[tile])
            scaled = [weight[level] * gap for level in range(tile_level + 1)]
            for level in range(inner):
                tab_ref[rows["inner"] + level, tile] = scaled[level]
            for group in range(TILE // GROUP):
                base = zero
                differ = block ^ group
                for level in range(inner, tile_level + 1):
                    least = 1 << (level - inner)
                    here = (differ >= least) & (differ < 2 * least) & (block > group)
                    base = jnp.where(here, scaled[level], base)
                tab_ref[rows["group"] + group, tile] = base
            tab_ref[rows["value"], tile] = jnp.exp(middles[tile] - local)
            if tile == low:
                tab_ref[rows["sibling"], tile] = zero
            else:
                tab_ref[rows["sibling"], tile] = weight[tile_level + 1] * jnp.exp(
                    local + totals[low] - middles[low]
                )
                local = local + totals[low]
            for bit in range(log2(pairs)):
                since = zero
                for other in range(pair >> bit << bit, pair):
                    since = since + pair_total[other]
                tab_ref[rows["state"] + bit, tile] = weight[tile_level + 2 + bit] * jnp.exp(
                    local + since
                )
            whole_decay = jnp.exp(local + running)
            first = log2(length) + 1
            for level in range(first, levels):
                far_ref[level - first, tile] = weight[level] * whole_decay
        pair_total.append(totals[low] + totals[low + 1])
        running = running + pair_total[-1]


def near_kernel(first_head, vt_ref, st_ref, tab_ref, kc_ref, qt_ref, *refs):
    near_ref, sc, mix, rest = refs[-4:]
    length = vt_ref.shape[1]
    width = vt_ref.shape[0] // STEP
    pairs = length // (2 * TILE)
    rows = table_rows(length)
    inner = log2(GROUP) + 1
    row = lax.broadcasted_iota(jnp.int32, (GROUP, TILE), 0)
    lane = lax.broadcasted_iota(jnp.int32, (GROUP, TILE), 1)
    within = lane % GROUP
    differ = row ^ within
    keys = state_keys(pairs)

    @pl.when(pl.program_id(0) == 0)
    def _():
        for pair in range(pairs):
            at = 2 * pair * TILE
            sc[pair] = jnp.dot(
                kc_ref[at : at + 2 * TILE, :],
                qt_ref[:, at : at + 2 * TILE],
                preferred_element_type=jnp.float32,
            ).astype(jnp.bfloat16)
            for place in range(STEP):
                mix[place, pair, TILE:, 0:TILE] = jnp.zeros((TILE, TILE), jnp.bfloat16)

    def one_head(place):
        head = first_head + pl.program_id(0) * STEP + place
        own = slice(place * width, (place + 1) * width)

        def table(order, tile):
            return tab_ref[order, tile, pl.ds(head, 1), :]

        for pair in range(pairs):
            at = 2 * pair * TILE
            for side in range(2):
                tile = 2 * pair + side
                diagonal = jnp.where(differ == 0, table(rows["inner"], tile), 0.0)
                for level in range(1, inner):
                    here = (differ >= 1 << (level - 1)) & (differ < 1 << level) & (row < within)
                    diagonal = jnp.where(here, table(rows["inner"] + level, tile), diagonal)
                lanes = slice(side * TILE, (side + 1) * TILE)
                for group in range(TILE // GROUP):
                    base = table(rows["group"] + group, tile)
                    weight = jnp.where(lane // GROUP == group, diagonal, base).astype(jnp.bfloat16)
                    start = side * TILE + group * GROUP
                    mix[place, pair, start : start + GROUP, lanes] = (
                        sc[pair, start : start + GROUP, lanes] * weight
                    )
            mix[place, pair, 0:TILE, TILE:] = sc[pair, 0:TILE, TILE:] * table(
                rows["sibling"], 2 * pair + 1
            ).astype(jnp.bfloat16)
            value = vt_ref[own, at : at + 2 * TILE] * pair_row(
                tab_ref.at[rows["value"]], head, pair
            ).astype(jnp.bfloat16)
            summed = jnp.dot(value, mix[place, pair], preferred_element_type=jnp.float32)
            active = [bit for bit in range(log2(pairs)) if pair >> bit & 1]
            if active:
                held = []
                for order, bit in enumerate(active):
                    scale = pair_row(tab_ref.at[rows["state"] + bit], head, pair).astype(jnp.bfloat16)
                    rest[place, pair, order * TILE : (order + 1) * TILE, :] = (
                        qt_ref[:, at : at + 2 * TILE] * scale
                    )
                    held.append(st_ref[keys.index((bit, pair >> bit + 1 << bit + 1)), own, :])
                summed = summed + jnp.dot(
                    jnp.concatenate(held, axis=1),
                    rest[place, pair, 0 : len(active) * TILE, :],
                    preferred_element_type=jnp.float32,
                )
            near_ref[own, at : at + 2 * TILE] = summed.astype(jnp.bfloat16)

    for place in range(STEP):
        one_head(place)


def far_kernel(place_ref, near_ref, own_ref, high_ref, far_ref, qt_ref, off_ref, gain_ref, *refs):
    out_ref, rest = refs[-2:]
    bits = far_ref.shape[0]
    length = qt_ref.shape[1]
    width = near_ref.shape[0] // STEP
    for place in range(STEP):
        own = slice(place * width, (place + 1) * width)
        head = (place_ref[0] + pl.program_id(0)) * STEP + place
        held = jnp.concatenate(
            [own_ref[own, :]] + [high_ref[bit, own, :] for bit in range(bits - 1)], axis=1
        )
        gain = jnp.broadcast_to(gain_ref[:, own], (TILE, TILE)).T
        factors = []
        for bit in range(bits):
            factor = jnp.exp(off_ref[bit, pl.ds(head, 1), :])
            factors.append(jnp.concatenate([factor, factor], axis=1))
        for pair in range(length // (2 * TILE)):
            at = 2 * pair * TILE
            for bit in range(bits):
                row = (pair_row(far_ref.at[bit], head, pair) * factors[bit]).astype(jnp.bfloat16)
                rest[place, pair, bit * TILE : (bit + 1) * TILE, :] = qt_ref[:, at : at + 2 * TILE] * row
            summed = near_ref[own, at : at + 2 * TILE].astype(jnp.float32) + jnp.dot(
                held, rest[place, pair], preferred_element_type=jnp.float32
            )
            mean = jnp.mean(summed * summed, axis=0, keepdims=True)
            normed = summed * lax.rsqrt(mean + EPSILON)
            for side in range(2):
                part = normed[:, side * TILE : (side + 1) * TILE] * gain
                start = at + side * TILE
                out_ref[start : start + TILE, own] = part.astype(jnp.bfloat16).T


def send(x, by, size):
    return lax.ppermute(x, "seq", [(i, i ^ by) for i in range(size)])


def shift(x, by, size):
    return lax.ppermute(x, "seq", [(i, i + by) for i in range(size - by)])


def at_rows(x, first, count):
    return lax.dynamic_slice_in_dim(x, first, count, 0)


def grow(decay, first, count, width):
    return jnp.repeat(jnp.exp(at_rows(decay, first, count)), width)[:, None]


def on_device(
    query_inputs, key_inputs, value_inputs, log_decay, level_weight, conv_weight, norm_gain
):
    length, state_dim = query_inputs.shape
    heads = log_decay.shape[0]
    values_dim = value_inputs.shape[1]
    width = values_dim // heads
    taps = conv_weight.shape[0]
    rim = taps - 1
    size = lax.axis_size("seq")
    bits = log2(size)
    pairs = length // (2 * TILE)
    keys = state_keys(pairs)
    half, quarter = values_dim // 2, values_dim // 4
    half_heads, quarter_heads = heads // 2, heads // 4
    tail = 4 * heads
    index = lax.axis_index("seq")
    core, side, plane = index & 1, index >> 1 & 1, index >> 2
    planes = size // 4
    rows = table_rows(length)
    calls = NEAR_CALLS if heads % NEAR_CALLS == 0 else 1
    each = heads // calls
    zero = jnp.zeros((heads,), jnp.float32)
    upper_core, upper_side = core == 1, side == 1

    own_rim = jnp.concatenate(
        [query_inputs[length - rim :], key_inputs[length - rim :], value_inputs[length - rim :]],
        axis=1,
    )
    rims = shift(own_rim, 1, size)

    tab, far_tab = pl.pallas_call(
        table_kernel,
        out_shape=[
            shape_of((rows["size"], length // TILE, heads, TILE), jnp.float32),
            shape_of((bits, length // TILE, heads, TILE), jnp.float32),
        ],
        cost_estimate=pl.CostEstimate(flops=10**9, bytes_accessed=3 * 10**6, transcendentals=0),
        name="tables",
    )(log_decay, level_weight)

    vt, st, group, qt, kc = pl.pallas_call(
        state_kernel,
        grid=(heads // STEP,),
        in_specs=[
            whole(query_inputs),
            whole(key_inputs),
            pl.BlockSpec((length, STEP * width), lambda i: (0, i)),
            pl.BlockSpec((rim, state_dim), lambda i: (0, 0)),
            pl.BlockSpec((rim, state_dim), lambda i: (0, 1)),
            pl.BlockSpec((rim, STEP * width), lambda i: (0, 2 * state_dim // (STEP * width) + i)),
            pl.BlockSpec((taps, state_dim), lambda i: (0, 0)),
            pl.BlockSpec((taps, state_dim), lambda i: (0, 1)),
            pl.BlockSpec((taps, STEP * width), lambda i: (0, 2 * state_dim // (STEP * width) + i)),
            whole(log_decay),
        ],
        out_specs=[
            pl.BlockSpec((STEP * width, length), lambda i: (i, 0)),
            pl.BlockSpec((len(keys), STEP * width, state_dim), lambda i: (0, i, 0)),
            pl.BlockSpec((values_dim + tail, state_dim), lambda i: (0, 0)),
            pl.BlockSpec((state_dim, length), lambda i: (0, 0)),
            pl.BlockSpec((length, state_dim), lambda i: (0, 0)),
        ],
        out_shape=[
            shape_of((values_dim, length), jnp.bfloat16),
            shape_of((len(keys), values_dim, state_dim), jnp.bfloat16),
            shape_of((values_dim + tail, state_dim), jnp.bfloat16),
            shape_of((state_dim, length), jnp.bfloat16),
            shape_of((length, state_dim), jnp.bfloat16),
        ],
        scratch_shapes=[
            pltpu.VMEM((STEP, length + 8, TILE), jnp.float32),
            pltpu.VMEM((length // TILE, heads, TILE), jnp.float32),
            pltpu.VMEM((pairs, heads, TILE), jnp.float32),
        ],
        cost_estimate=pl.CostEstimate(flops=10**9, bytes_accessed=9 * 10**6, transcendentals=0),
        name="state",
    )(
        query_inputs, key_inputs, value_inputs, rims, rims, rims,
        conv_weight, conv_weight, conv_weight, log_decay,
    )

    near = None
    for call in range(calls):
        first = call * each // STEP
        before = [] if near is None else [near]
        near = pl.pallas_call(
            functools.partial(near_kernel, call * each),
            grid=(each // STEP,),
            in_specs=[
                pl.BlockSpec((STEP * width, length), lambda i, first=first: (first + i, 0)),
                pl.BlockSpec(
                    (len(keys), STEP * width, state_dim), lambda i, first=first: (0, first + i, 0)
                ),
                whole(tab),
                whole(kc),
                whole(qt),
            ]
            + [pl.BlockSpec(memory_space=pl.ANY) for _ in before],
            out_specs=pl.BlockSpec((STEP * width, length), lambda i, first=first: (first + i, 0)),
            out_shape=shape_of((values_dim, length), jnp.bfloat16),
            scratch_shapes=[
                pltpu.VMEM((pairs, 2 * TILE, 2 * TILE), jnp.bfloat16),
                pltpu.VMEM((STEP, pairs, 2 * TILE, 2 * TILE), jnp.bfloat16),
                pltpu.VMEM((STEP, pairs, log2(pairs) * state_dim, 2 * TILE), jnp.bfloat16),
            ],
            input_output_aliases={5: 0} if before else {},
            cost_estimate=pl.CostEstimate(flops=10**9, bytes_accessed=4 * 10**6, transcendentals=0),
            name="near",
        )(vt, st, tab, kc, qt, *before)

    other = send(group, 1, size)
    total = sum_terms(group[values_dim:])[:, 0]
    other_total = sum_terms(other[values_dim:])[:, 0]
    first_head = core * half_heads
    own_half = at_rows(group, core * half, half).astype(jnp.float32)
    other_half = at_rows(other, core * half, half).astype(jnp.float32)
    chip = jnp.where(
        upper_core,
        own_half + grow(total, first_head, half_heads, width) * other_half,
        other_half + grow(other_total, first_head, half_heads, width) * own_half,
    ).astype(jnp.bfloat16)
    chip_total = total + other_total
    in_chip = jnp.where(upper_core, other_total, zero)
    offsets = [jnp.where(upper_core, zero, NEVER), jnp.where(upper_side, in_chip, NEVER)]

    def with_total(state, decay):
        wide = jnp.broadcast_to(decay[:, None], (heads, state_dim))
        return jnp.concatenate([state, three_terms(wide)], axis=0)

    mine = at_rows(chip, side * quarter, quarter)
    theirs = at_rows(chip, (1 - side) * quarter, quarter)
    got = send(with_total(theirs, chip_total), 2, size)
    got_rest = send(mine, 2, size)
    got_mine, got_total = got[:quarter], sum_terms(got[quarter:])[:, 0]
    my_head = first_head + side * quarter_heads
    mine_wide, got_wide = mine.astype(jnp.float32), got_mine.astype(jnp.float32)
    flat = jnp.where(
        upper_side,
        mine_wide + grow(chip_total, my_head, quarter_heads, width) * got_wide,
        got_wide + grow(got_total, my_head, quarter_heads, width) * mine_wide,
    ).astype(jnp.bfloat16)
    in_plane = in_chip + jnp.where(upper_side, got_total, zero)

    message = with_total(flat, chip_total + got_total)
    came = []
    for by in range(1, planes):
        came.append(shift(message, 4 * by, size))
    parts = []
    for bit in range(log2(planes)):
        summed = jnp.zeros((quarter, state_dim), jnp.float32)
        between = zero
        upper = plane >> bit & 1 == 1
        for by in range(1, planes):
            source = plane - by
            here = (
                upper
                & (source >= 0)
                & (source >> (bit + 1) == plane >> (bit + 1))
                & (source >> bit & 1 == 0)
            )
            factor = grow(jnp.where(here, between, NEVER), my_head, quarter_heads, width)
            summed = summed + factor * came[by - 1][:quarter].astype(jnp.float32)
            between = between + sum_terms(came[by - 1][quarter:])[:, 0]
        parts.append(summed.astype(jnp.bfloat16))
        offsets.append(jnp.where(upper, in_plane, NEVER))

    halves = [jnp.concatenate([got_rest, got_mine], axis=0)[None]]
    if parts:
        part = jnp.stack(parts)
        swapped = send(part, 2, size)
        halves.append(
            jnp.where(
                upper_side,
                jnp.concatenate([swapped, part], axis=1),
                jnp.concatenate([part, swapped], axis=1),
            )
        )
    high = jnp.concatenate(halves, axis=0)
    high_other = send(high, 1, size)

    off = jnp.broadcast_to(jnp.stack(offsets)[:, :, None], (bits, heads, TILE))
    gain = norm_gain.reshape(1, values_dim)
    out = None
    for first, states in ((core, high), (1 - core, high_other)):
        before = [] if out is None else [out]
        out = pl.pallas_call(
            far_kernel,
            grid_spec=pltpu.PrefetchScalarGridSpec(
                num_scalar_prefetch=1,
                grid=(half_heads // STEP,),
                in_specs=[
                    pl.BlockSpec((STEP * width, length), lambda i, s: (s[0] + i, 0)),
                    pl.BlockSpec((STEP * width, state_dim), lambda i, s: (s[0] + i, 0)),
                    pl.BlockSpec((bits - 1, STEP * width, state_dim), lambda i, s: (0, i, 0)),
                    pl.BlockSpec(far_tab.shape, lambda i, s: (0, 0, 0, 0)),
                    pl.BlockSpec(qt.shape, lambda i, s: (0, 0)),
                    pl.BlockSpec(off.shape, lambda i, s: (0, 0, 0)),
                    pl.BlockSpec((1, STEP * width), lambda i, s: (0, s[0] + i)),
                ]
                + [pl.BlockSpec(memory_space=pl.ANY) for _ in before],
                out_specs=pl.BlockSpec((length, STEP * width), lambda i, s: (0, s[0] + i)),
                scratch_shapes=[pltpu.VMEM((STEP, pairs, bits * state_dim, 2 * TILE), jnp.bfloat16)],
            ),
            out_shape=shape_of((length, values_dim), jnp.bfloat16),
            input_output_aliases={8: 0} if before else {},
            cost_estimate=pl.CostEstimate(flops=10**9, bytes_accessed=6 * 10**6, transcendentals=0),
            name="far",
        )((first * half_heads // STEP)[None], near, other, states, far_tab, qt, off, gain, *before)
    return out


def solution(mesh):
    return jax.shard_map(
        on_device,
        mesh=mesh,
        in_specs=(
            P(("grp", "seq"), None),
            P(("grp", "seq"), None),
            P(("grp", "seq"), None),
            P(None, ("grp", "seq")),
            P(None, None, ("grp", "seq")),
            P(),
            P(),
        ),
        out_specs=P(("grp", "seq"), None),
        check_vma=False,
    )
```

```python
import functools

import jax
import jax.numpy as jnp
from jax import lax
from jax.experimental import pallas as pl
from jax.experimental.pallas import tpu as pltpu
from jax.sharding import PartitionSpec as P


EPSILON = 1e-05
TILE = 128
GROUP = 16
NEAR_CALLS = (4, 12)
STEP = 2


def log2(value):
    return value.bit_length() - 1


def whole(array):
    rank = array.ndim
    return pl.BlockSpec(array.shape, lambda i: (0,) * rank)


def shape_of(shape, dtype):
    return jax.ShapeDtypeStruct(shape, dtype)


RESIDENT = pl.BlockSpec(memory_space=pltpu.VMEM)
PARAMS = pltpu.CompilerParams(vmem_limit_bytes=24 << 20)


def rows_of(head, width):
    return pl.ds(pl.multiple_of(head * width, width), width)


def tile_decays(log_decay):
    length = log_decay.shape[1]
    row = lax.broadcasted_iota(jnp.int32, (TILE, TILE), 0)
    col = lax.broadcasted_iota(jnp.int32, (TILE, TILE), 1)
    parts = [log_decay[:, at : at + TILE] for at in range(0, length, TILE)]
    local = lax.dot_general(
        jnp.concatenate(parts, axis=0),
        (row <= col).astype(jnp.float32),
        (((1,), (0,)), ((), ())),
        precision=lax.Precision.HIGHEST,
        preferred_element_type=jnp.float32,
    )
    middle = jnp.broadcast_to(local[:, TILE // 2 - 1 : TILE // 2], local.shape)
    total = jnp.broadcast_to(local[:, TILE - 1 : TILE], local.shape)
    heads = log_decay.shape[0]

    def split(array):
        return [array[at : at + heads] for at in range(0, array.shape[0], heads)]

    return split(local), split(middle), split(total)


def pair_row(table, head, pair):
    sides = [table[2 * pair + side, pl.ds(head, 1), :] for side in range(2)]
    return jnp.concatenate(sides, axis=1)


def conv_tile(buf, weight, start):
    taps = weight.shape[0]
    total = None
    for tap in range(taps):
        term = weight[tap : tap + 1, :] * buf[pl.ds(8 - (taps - 1) + tap + start, TILE), :]
        total = term if total is None else total + term
    return total + total * jnp.tanh(total)


def fill(buf, source, rim):
    length = source.shape[0]
    buf[pl.ds(8 - rim.shape[0], rim.shape[0]), :] = rim[...].astype(jnp.float32)
    buf[pl.ds(8, length), :] = source[...].astype(jnp.float32)


def state_keys(pairs):
    return [
        (bit, first)
        for bit in range(log2(pairs))
        for first in range(0, pairs, 2 << bit)
    ]


def three_terms(wide):
    terms = []
    for _ in range(3):
        term = wide.astype(jnp.bfloat16)
        terms.append(term)
        wide = wide - term.astype(jnp.float32)
    terms.append(jnp.zeros_like(terms[0]))
    return jnp.concatenate(terms, axis=0)


def sum_terms(terms):
    each = terms.shape[0] // 4
    wide = terms.astype(jnp.float32)
    return wide[:each] + wide[each : 2 * each] + wide[2 * each : 3 * each]


def state_kernel(
    q_ref, k_ref, v_ref, rq_ref, rk_ref, rv_ref, wq_ref, wk_ref, wv_ref, ld_ref,
    vt_ref, st_ref, g_ref, qt_ref, kc_ref,
    buf, scale, total,
):
    step = pl.program_id(0)
    heads = ld_ref.shape[0]
    length = v_ref.shape[0]
    width = v_ref.shape[1] // STEP
    pairs = length // (2 * TILE)

    @pl.when(step == 0)
    def _():
        local, _, totals = tile_decays(ld_ref[...])
        summed = None
        for pair in range(pairs):
            low, high = 2 * pair, 2 * pair + 1
            scale[low] = jnp.exp(totals[low] - local[low] + totals[high])
            scale[high] = jnp.exp(totals[high] - local[high])
            both = totals[low] + totals[high]
            total[pair] = jnp.exp(both)
            summed = both if summed is None else summed + both
        g_ref[pl.ds(heads * width, 4 * heads), :] = three_terms(summed)
        fill(buf.at[0], q_ref, rq_ref)
        fill(buf.at[1], k_ref, rk_ref)
        for tile in range(length // TILE):
            at = tile * TILE
            done = conv_tile(buf.at[0], 0.5 * wq_ref[...], at).astype(jnp.bfloat16)
            qt_ref[:, at : at + TILE] = done.T
            kc_ref[at : at + TILE, :] = conv_tile(buf.at[1], 0.5 * wk_ref[...], at).astype(jnp.bfloat16)

    for place in range(STEP):
        lanes = slice(place * width, (place + 1) * width)
        fill(buf.at[place], v_ref.at[:, lanes], rv_ref.at[:, lanes])
    for place in range(STEP):
        head = step * STEP + place
        lanes = slice(place * width, (place + 1) * width)
        weight = 0.5 * wv_ref[:, lanes]
        states = {}
        for pair in range(pairs):
            at = 2 * pair * TILE
            sides = []
            for start in (at, at + TILE):
                done = conv_tile(buf.at[place], weight, start).astype(jnp.bfloat16).T
                vt_ref[rows_of(head, width), start : start + TILE] = done
                sides.append(done)
            row = pair_row(scale, head, pair).astype(jnp.bfloat16)
            states[(0, pair)] = jnp.dot(
                jnp.concatenate(sides, axis=1) * row,
                kc_ref[at : at + 2 * TILE, :],
                preferred_element_type=jnp.float32,
            )
        decay = [total[pair, pl.ds(head, 1), :] for pair in range(pairs)]
        for bit in range(log2(pairs)):
            for first in range(0, pairs, 2 << bit):
                keep = states[(bit, first + (1 << bit))]
                factor = decay[first + (1 << bit)]
                for later in range(first + (1 << bit) + 1, first + (2 << bit)):
                    factor = factor * decay[later]
                states[(bit + 1, first)] = keep + factor * states[(bit, first)]
        for order, key in enumerate(state_keys(pairs)):
            st_ref[order, rows_of(head, width), :] = states[key].astype(jnp.bfloat16)
        g_ref[rows_of(head, width), :] = states[(log2(pairs), 0)].astype(jnp.bfloat16)


def table_rows(length):
    inner = log2(GROUP) + 1
    groups = TILE // GROUP
    states = log2(length // (2 * TILE))
    return {
        "inner": 0,
        "group": inner,
        "sibling": inner + groups,
        "value": inner + groups + 1,
        "state": inner + groups + 2,
        "size": inner + groups + 2 + states,
    }


def table_kernel(ld_ref, lw_ref, tab_ref, far_ref):
    heads, length = ld_ref.shape
    levels = lw_ref.shape[0]
    pairs = length // (2 * TILE)
    rows = table_rows(length)
    inner = log2(GROUP) + 1
    tile_level = log2(TILE)
    locals_, middles, totals = tile_decays(ld_ref[...])
    block = lax.broadcasted_iota(jnp.int32, (heads, TILE), 1) // GROUP
    zero = jnp.zeros((heads, TILE), jnp.float32)
    pair_total = []
    running = zero
    for pair in range(pairs):
        low = 2 * pair
        for tile in (low, low + 1):
            lanes = pl.ds(tile * TILE, TILE)
            weight = [lw_ref[level, :, lanes].astype(jnp.float32) for level in range(levels)]
            local = locals_[tile]
            gap = jnp.exp(local - middles[tile])
            scaled = [weight[level] * gap for level in range(tile_level + 1)]
            for level in range(inner):
                tab_ref[rows["inner"] + level, tile] = scaled[level]
            for group in range(TILE // GROUP):
                base = zero
                differ = block ^ group
                for level in range(inner, tile_level + 1):
                    least = 1 << (level - inner)
                    here = (differ >= least) & (differ < 2 * least) & (block > group)
                    base = jnp.where(here, scaled[level], base)
                tab_ref[rows["group"] + group, tile] = base
            tab_ref[rows["value"], tile] = jnp.exp(middles[tile] - local)
            if tile == low:
                tab_ref[rows["sibling"], tile] = zero
            else:
                tab_ref[rows["sibling"], tile] = weight[tile_level + 1] * jnp.exp(
                    local + totals[low] - middles[low]
                )
                local = local + totals[low]
            for bit in range(log2(pairs)):
                since = zero
                for other in range(pair >> bit << bit, pair):
                    since = since + pair_total[other]
                tab_ref[rows["state"] + bit, tile] = weight[tile_level + 2 + bit] * jnp.exp(
                    local + since
                )
            whole_decay = jnp.exp(local + running)
            first = log2(length) + 1
            for level in range(first, levels):
                far_ref[level - first, tile] = weight[level] * whole_decay
        pair_total.append(totals[low] + totals[low + 1])
        running = running + pair_total[-1]


def rim_kernel(place_ref, q_ref, k_ref, v_ref, out_ref):
    rows, state_dim = out_ref.shape[0], q_ref.shape[1]
    last = slice(q_ref.shape[0] - rows, q_ref.shape[0])
    out_ref[:, 0:state_dim] = q_ref[last, :]
    out_ref[:, state_dim : 2 * state_dim] = k_ref[last, :]
    out_ref[:, 2 * state_dim :] = v_ref[last, :]


def score_kernel(qt_ref, kc_ref, sc_ref):
    for pair in range(sc_ref.shape[0]):
        at = 2 * pair * TILE
        sc_ref[pair] = jnp.dot(
            kc_ref[at : at + 2 * TILE, :],
            qt_ref[:, at : at + 2 * TILE],
            preferred_element_type=jnp.float32,
        ).astype(jnp.bfloat16)


def near_kernel(first_head, width, vt_ref, st_ref, tab_ref, sc, qt_ref, near_ref, mix, rest):
    length = vt_ref.shape[1]
    pairs = length // (2 * TILE)
    rows = table_rows(length)
    inner = log2(GROUP) + 1
    row = lax.broadcasted_iota(jnp.int32, (GROUP, TILE), 0)
    lane = lax.broadcasted_iota(jnp.int32, (GROUP, TILE), 1)
    within = lane % GROUP
    differ = row ^ within
    keys = state_keys(pairs)

    @pl.when(pl.program_id(0) == 0)
    def _():
        for pair in range(pairs):
            for place in range(STEP):
                mix[place, pair, TILE:, 0:TILE] = jnp.zeros((TILE, TILE), jnp.bfloat16)

    def one_head(place):
        head = first_head + pl.program_id(0) * STEP + place
        own = rows_of(head, width)

        def table(order, tile):
            return tab_ref[order, tile, pl.ds(head, 1), :]

        for pair in range(pairs):
            at = 2 * pair * TILE
            for side in range(2):
                tile = 2 * pair + side
                diagonal = jnp.where(differ == 0, table(rows["inner"], tile), 0.0)
                for level in range(1, inner):
                    here = (differ >= 1 << (level - 1)) & (differ < 1 << level) & (row < within)
                    diagonal = jnp.where(here, table(rows["inner"] + level, tile), diagonal)
                lanes = slice(side * TILE, (side + 1) * TILE)
                for group in range(TILE // GROUP):
                    base = table(rows["group"] + group, tile)
                    weight = jnp.where(lane // GROUP == group, diagonal, base).astype(jnp.bfloat16)
                    start = side * TILE + group * GROUP
                    mix[place, pair, start : start + GROUP, lanes] = (
                        sc[pair, start : start + GROUP, lanes] * weight
                    )
            mix[place, pair, 0:TILE, TILE:] = sc[pair, 0:TILE, TILE:] * table(
                rows["sibling"], 2 * pair + 1
            ).astype(jnp.bfloat16)
            value = vt_ref[own, at : at + 2 * TILE] * pair_row(
                tab_ref.at[rows["value"]], head, pair
            ).astype(jnp.bfloat16)
            summed = jnp.dot(value, mix[place, pair], preferred_element_type=jnp.float32)
            active = [bit for bit in range(log2(pairs)) if pair >> bit & 1]
            if active:
                held = []
                for order, bit in enumerate(active):
                    scale = pair_row(tab_ref.at[rows["state"] + bit], head, pair).astype(jnp.bfloat16)
                    rest[place, pair, order * TILE : (order + 1) * TILE, :] = (
                        qt_ref[:, at : at + 2 * TILE] * scale
                    )
                    held.append(st_ref[keys.index((bit, pair >> bit + 1 << bit + 1)), own, :])
                summed = summed + jnp.dot(
                    jnp.concatenate(held, axis=1),
                    rest[place, pair, 0 : len(active) * TILE, :],
                    preferred_element_type=jnp.float32,
                )
            near_ref[own, at : at + 2 * TILE] = summed.astype(jnp.bfloat16)

    for place in range(STEP):
        one_head(place)


def add_far(levels, head, width, near_ref, buckets, far_ref, qt_ref, off_ref, rest, finish):
    length = qt_ref.shape[1]
    held = jnp.concatenate(buckets, axis=1)
    factors = []
    for level in levels:
        factor = off_ref[level, pl.ds(head, 1), :]
        factors.append(jnp.concatenate([factor, factor], axis=1))
    for pair in range(length // (2 * TILE)):
        at = 2 * pair * TILE
        for order, level in enumerate(levels):
            row = (pair_row(far_ref.at[level], head, pair) * factors[order]).astype(jnp.bfloat16)
            rest[pair, order * TILE : (order + 1) * TILE, :] = qt_ref[:, at : at + 2 * TILE] * row
        summed = near_ref[rows_of(head, width), at : at + 2 * TILE].astype(jnp.float32) + jnp.dot(
            held, rest[pair], preferred_element_type=jnp.float32
        )
        finish(at, summed)


def mid_kernel(
    width, place_ref, near_ref, chip_ref, low_ref, low_other_ref, far_ref, qt_ref, off_ref, out_ref, rest
):
    step, steps = pl.program_id(0), pl.num_programs(0)
    for place in range(STEP):
        own = slice(place * width, (place + 1) * width)
        head = lax.rem(place_ref[0] * (steps // 2) + step, steps) * STEP + place
        low = jnp.where(step < steps // 2, low_ref[own, :], low_other_ref[own, :])

        def finish(at, summed, head=head):
            out_ref[rows_of(head, width), at : at + 2 * TILE] = summed.astype(jnp.bfloat16)

        add_far(
            (0, 1), head, width, near_ref, [chip_ref[own, :], low], far_ref, qt_ref, off_ref, rest.at[place], finish
        )


def far_kernel(width, other, place_ref, near_ref, high_ref, far_ref, qt_ref, off_ref, gain_ref, *refs):
    out_ref, rest = refs[-2:]
    count = high_ref.shape[0]
    for place in range(STEP):
        own = slice(place * width, (place + 1) * width)
        core = 1 - place_ref[0] if other else place_ref[0]
        head = (core * pl.num_programs(0) + pl.program_id(0)) * STEP + place
        gain = jnp.broadcast_to(gain_ref[:, own], (TILE, TILE)).T

        def finish(at, summed, own=own, gain=gain):
            mean = jnp.mean(summed * summed, axis=0, keepdims=True)
            normed = summed * lax.rsqrt(mean + EPSILON)
            for side in range(2):
                part = normed[:, side * TILE : (side + 1) * TILE] * gain
                start = at + side * TILE
                out_ref[start : start + TILE, own] = part.astype(jnp.bfloat16).T

        add_far(
            tuple(range(2, 2 + count)),
            head,
            width,
            near_ref,
            [high_ref[level, own, :] for level in range(count)],
            far_ref,
            qt_ref,
            off_ref,
            rest.at[place],
            finish,
        )


def core_kernel(width, place_ref, own_ref, other_ref, theirs_ref, mine_ref, keep_ref, factor):
    heads = keep_ref.shape[1]
    states = heads * width
    quarter = heads // 4
    core, side = place_ref[0], place_ref[1]
    upper = core == 1
    own_total = sum_terms(own_ref[states:, :])
    other_total = sum_terms(other_ref[states:, :])
    factor[...] = jnp.exp(jnp.where(upper, own_total, other_total))
    keep_ref[0] = own_total + other_total
    keep_ref[1] = jnp.where(upper, other_total, 0.0)
    for out_ref, column in ((theirs_ref, 1 - side), (mine_ref, side)):
        for order in range(quarter):
            head = (core * 2 + column) * quarter + order
            own = own_ref[rows_of(head, width), :].astype(jnp.float32)
            other = other_ref[rows_of(head, width), :].astype(jnp.float32)
            scale = factor[pl.ds(head, 1), :]
            last, first = jnp.where(upper, own, other), jnp.where(upper, other, own)
            out_ref[order * width : (order + 1) * width, :] = (last + scale * first).astype(jnp.bfloat16)
    theirs_ref[quarter * width :, :] = three_terms(own_total + other_total)


def side_kernel(width, place_ref, got_ref, mine_ref, chip_ref, message_ref, keep_ref, factor):
    heads = keep_ref.shape[1]
    quarter = heads // 4
    core, side = place_ref[0], place_ref[1]
    upper = side == 1
    chip_total = chip_ref[0]
    got_total = sum_terms(got_ref[quarter * width :, :])
    factor[...] = jnp.exp(jnp.where(upper, chip_total, got_total))
    keep_ref[0] = chip_ref[1]
    keep_ref[1] = chip_ref[1] + jnp.where(upper, got_total, 0.0)
    for order in range(quarter):
        rows = slice(order * width, (order + 1) * width)
        mine, got = mine_ref[rows, :].astype(jnp.float32), got_ref[rows, :].astype(jnp.float32)
        scale = factor[pl.ds((core * 2 + side) * quarter + order, 1), :]
        last, first = jnp.where(upper, mine, got), jnp.where(upper, got, mine)
        message_ref[rows, :] = (last + scale * first).astype(jnp.bfloat16)
    message_ref[quarter * width :, :] = three_terms(chip_total + got_total)


def plane_kernel(width, place_ref, *refs):
    far_ref, part_ref, factor = refs[-3:]
    came, keep_ref = refs[:-4], refs[-4]
    heads = keep_ref.shape[1]
    quarter = heads // 4
    core, side, plane = place_ref[0], place_ref[1], place_ref[2]
    planes = len(came) + 1
    totals = [sum_terms(ref[quarter * width :, :]) for ref in came]
    zero = jnp.zeros_like(totals[0])
    far_ref[0] = jnp.where(core == 1, jnp.ones_like(zero), 0.0)
    far_ref[1] = jnp.where(side == 1, jnp.exp(keep_ref[0]), 0.0)
    in_plane = jnp.exp(keep_ref[1])
    for bit in range(log2(planes)):
        upper = (plane >> bit) & 1 == 1
        far_ref[2 + bit] = jnp.where(upper, in_plane, 0.0)
        for by in range(1, planes):
            source = plane ^ by
            here = upper & (source >> (bit + 1) == plane >> (bit + 1)) & ((source >> bit) & 1 == 0)
            between = zero
            for mid in range(1, planes):
                inside = (plane ^ mid > source) & (plane ^ mid < plane)
                between = between + jnp.where(inside, totals[mid - 1], 0.0)
            factor[by - 1] = jnp.where(here, jnp.exp(between), 0.0)
        for order in range(quarter):
            rows = slice(order * width, (order + 1) * width)
            head = (core * 2 + side) * quarter + order
            summed = None
            for by in range(1, planes):
                term = factor[by - 1, pl.ds(head, 1), :] * came[by - 1][rows, :].astype(jnp.float32)
                summed = term if summed is None else summed + term
            part_ref[bit, rows, :] = summed.astype(jnp.bfloat16)


def stack_kernel(first_ref, last_ref, out_ref):
    half = first_ref.shape[0]
    out_ref[0:half, :] = first_ref[...]
    out_ref[half:, :] = last_ref[0:half, :]


def column_kernel(place_ref, part_ref, swapped_ref, out_ref):
    side = place_ref[1]
    count, quarter, _ = part_ref.shape
    for level in range(count):
        out_ref[level, rows_of(side, quarter), :] = part_ref[level]
        out_ref[level, rows_of(1 - side, quarter), :] = swapped_ref[level]


def glue(kernel, out_shape, scratch=()):
    scalar = pl.BlockSpec(memory_space=pltpu.SMEM)

    def call(*args, place=None):
        first = [] if place is None else [place]
        many = isinstance(out_shape, list)
        return pl.pallas_call(
            kernel,
            in_specs=[scalar for _ in first] + [RESIDENT for _ in args],
            out_specs=[RESIDENT for _ in out_shape] if many else RESIDENT,
            out_shape=out_shape,
            scratch_shapes=list(scratch),
            compiler_params=PARAMS,
            cost_estimate=pl.CostEstimate(flops=10**7, bytes_accessed=10**6, transcendentals=0),
        )(*first, *args)

    return call


def send(x, by, size):
    return lax.ppermute(x, "seq", [(i, i ^ by) for i in range(size)])


def shift(x, by, size):
    return lax.ppermute(x, "seq", [(i, i + by) for i in range(size - by)])


def on_device(
    query_inputs, key_inputs, value_inputs, log_decay, level_weight, conv_weight, norm_gain
):
    length, state_dim = query_inputs.shape
    heads = log_decay.shape[0]
    values_dim = value_inputs.shape[1]
    width = values_dim // heads
    taps = conv_weight.shape[0]
    rim = taps - 1
    size = lax.axis_size("seq")
    bits = log2(size)
    pairs = length // (2 * TILE)
    keys = state_keys(pairs)
    half, quarter = values_dim // 2, values_dim // 4
    half_heads = heads // 2
    tail = 4 * heads
    index = lax.axis_index("seq")
    core = index & 1
    place = jnp.stack([core, index >> 1 & 1, index >> 2]).astype(jnp.int32)
    half_steps = half_heads // STEP
    gain = norm_gain.reshape(1, values_dim)
    planes = size // 4
    rows = table_rows(length)
    calls = NEAR_CALLS if sum(NEAR_CALLS) == heads else (heads,)

    last = length // GROUP - 1
    own_rim = pl.pallas_call(
        rim_kernel,
        grid=(1,),
        in_specs=[pl.BlockSpec(memory_space=pltpu.SMEM)]
        + [pl.BlockSpec((GROUP, x.shape[1]), lambda i: (last, 0)) for x in (query_inputs, key_inputs, value_inputs)],
        out_specs=pl.BlockSpec((rim, 2 * state_dim + values_dim), lambda i: (0, 0)),
        out_shape=shape_of((rim, 2 * state_dim + values_dim), jnp.bfloat16),
        name="rim",
    )(place, query_inputs, key_inputs, value_inputs)
    rims = shift(own_rim, 1, size)

    tab, far_tab = pl.pallas_call(
        table_kernel,
        out_specs=[RESIDENT] * 2,
        out_shape=[
            pltpu.VMEM((rows["size"], length // TILE, heads, TILE), jnp.float32),
            pltpu.VMEM((bits, length // TILE, heads, TILE), jnp.float32),
        ],
        compiler_params=PARAMS,
        cost_estimate=pl.CostEstimate(flops=10**9, bytes_accessed=3 * 10**6, transcendentals=0),
        name="tables",
    )(log_decay, level_weight)

    vt, st, group, qt, kc = pl.pallas_call(
        state_kernel,
        grid=(heads // STEP,),
        in_specs=[
            whole(query_inputs),
            whole(key_inputs),
            pl.BlockSpec((length, STEP * width), lambda i: (0, i)),
            pl.BlockSpec((rim, state_dim), lambda i: (0, 0)),
            pl.BlockSpec((rim, state_dim), lambda i: (0, 1)),
            pl.BlockSpec((rim, STEP * width), lambda i: (0, 2 * state_dim // (STEP * width) + i)),
            pl.BlockSpec((taps, state_dim), lambda i: (0, 0)),
            pl.BlockSpec((taps, state_dim), lambda i: (0, 1)),
            pl.BlockSpec((taps, STEP * width), lambda i: (0, 2 * state_dim // (STEP * width) + i)),
            whole(log_decay),
        ],
        out_specs=[RESIDENT] * 5,
        out_shape=[
            pltpu.VMEM((values_dim, length), jnp.bfloat16),
            pltpu.VMEM((len(keys), values_dim, state_dim), jnp.bfloat16),
            pltpu.VMEM((values_dim + tail, state_dim), jnp.bfloat16),
            pltpu.VMEM((state_dim, length), jnp.bfloat16),
            pltpu.VMEM((length, state_dim), jnp.bfloat16),
        ],
        scratch_shapes=[
            pltpu.VMEM((STEP, length + 8, TILE), jnp.float32),
            pltpu.VMEM((length // TILE, heads, TILE), jnp.float32),
            pltpu.VMEM((pairs, heads, TILE), jnp.float32),
        ],
        compiler_params=pltpu.CompilerParams(vmem_limit_bytes=52 << 20),
        cost_estimate=pl.CostEstimate(flops=10**9, bytes_accessed=9 * 10**6, transcendentals=0),
        name="state",
    )(
        query_inputs, key_inputs, value_inputs, rims, rims, rims,
        conv_weight, conv_weight, conv_weight, log_decay,
    )

    sc = pl.pallas_call(
        score_kernel,
        in_specs=[RESIDENT] * 2,
        out_specs=RESIDENT,
        out_shape=pltpu.VMEM((pairs, 2 * TILE, 2 * TILE), jnp.bfloat16),
        compiler_params=PARAMS,
        cost_estimate=pl.CostEstimate(flops=10**8, bytes_accessed=10**6, transcendentals=0),
        name="scores",
    )(qt, kc)

    near = vt
    for call, each in enumerate(calls):
        near = pl.pallas_call(
            functools.partial(near_kernel, sum(calls[:call]), width),
            grid=(each // STEP,),
            in_specs=[RESIDENT] * 5,
            out_specs=RESIDENT,
            out_shape=pltpu.VMEM((values_dim, length), jnp.bfloat16),
            scratch_shapes=[
                pltpu.VMEM((STEP, pairs, 2 * TILE, 2 * TILE), jnp.bfloat16),
                pltpu.VMEM((STEP, pairs, log2(pairs) * state_dim, 2 * TILE), jnp.bfloat16),
            ],
            input_output_aliases={0: 0},
            compiler_params=PARAMS,
            cost_estimate=pl.CostEstimate(flops=10**9, bytes_accessed=4 * 10**6, transcendentals=0),
            name="near",
        )(near, st, tab, sc, qt)

    other = send(group, 1, size)
    table = pltpu.VMEM((heads, state_dim), jnp.float32)
    message_shape = pltpu.VMEM((quarter + tail, state_dim), jnp.bfloat16)
    theirs, mine, keep = glue(
        functools.partial(core_kernel, width),
        [message_shape, pltpu.VMEM((quarter, state_dim), jnp.bfloat16), pltpu.VMEM((2, heads, state_dim), jnp.float32)],
        [table],
    )(group, other, place=place)

    got = send(theirs, 2, size)
    got_rest = send(mine, 2, size)
    message, keep = glue(
        functools.partial(side_kernel, width), [message_shape, pltpu.VMEM((2, heads, state_dim), jnp.float32)], [table]
    )(got, mine, keep, place=place)

    came = []
    for by in range(1, planes):
        came.append(send(message, 4 * by, size))

    low = glue(stack_kernel, pltpu.VMEM((half, state_dim), jnp.bfloat16))(got_rest, got)
    low_other = send(low, 1, size)

    count = bits - 2
    far_factor, part = glue(
        functools.partial(plane_kernel, width),
        [
            pltpu.VMEM((bits, heads, state_dim), jnp.float32),
            pltpu.VMEM((count, quarter, state_dim), jnp.bfloat16),
        ],
        [pltpu.VMEM((planes - 1, heads, state_dim), jnp.float32)],
    )(*came, keep, place=place)

    near = pl.pallas_call(
        functools.partial(mid_kernel, width),
        grid_spec=pltpu.PrefetchScalarGridSpec(
            num_scalar_prefetch=1,
            grid=(2 * half_steps,),
            in_specs=[
                RESIDENT,
                pl.BlockSpec((STEP * width, state_dim), lambda i, s: (lax.rem(s[0] * half_steps + i, 2 * half_steps), 0)),
                pl.BlockSpec((STEP * width, state_dim), lambda i, s: (jnp.minimum(i, half_steps - 1), 0)),
                pl.BlockSpec((STEP * width, state_dim), lambda i, s: (jnp.maximum(i - half_steps, 0), 0)),
                RESIDENT,
                RESIDENT,
                RESIDENT,
            ],
            out_specs=RESIDENT,
            scratch_shapes=[pltpu.VMEM((STEP, pairs, 2 * state_dim, 2 * TILE), jnp.bfloat16)],
        ),
        out_shape=pltpu.VMEM((values_dim, length), jnp.bfloat16),
        input_output_aliases={1: 0},
        compiler_params=PARAMS,
        cost_estimate=pl.CostEstimate(flops=10**9, bytes_accessed=6 * 10**6, transcendentals=0),
        name="mid",
    )(place, near, other, low, low_other, far_tab, qt, far_factor)

    swapped = send(part, 2, size)
    high = glue(column_kernel, pltpu.VMEM((count, half, state_dim), jnp.bfloat16))(part, swapped, place=place)
    high_other = send(high, 1, size)

    out = None
    for call, states in enumerate((high, high_other)):
        before = [] if out is None else [out]

        def columns(i, s, other=call):
            return (0, (1 - s[0] if other else s[0]) * half_steps + i)

        out = pl.pallas_call(
            functools.partial(far_kernel, width, call),
            grid_spec=pltpu.PrefetchScalarGridSpec(
                num_scalar_prefetch=1,
                grid=(half_steps,),
                in_specs=[
                    RESIDENT,
                    pl.BlockSpec((count, STEP * width, state_dim), lambda i, s: (0, i, 0)),
                    RESIDENT,
                    RESIDENT,
                    RESIDENT,
                    pl.BlockSpec((1, STEP * width), columns),
                ]
                + [pl.BlockSpec(memory_space=pl.ANY) for _ in before],
                out_specs=pl.BlockSpec((length, STEP * width), columns),
                scratch_shapes=[pltpu.VMEM((STEP, pairs, count * state_dim, 2 * TILE), jnp.bfloat16)],
            ),
            out_shape=shape_of((length, values_dim), jnp.bfloat16),
            input_output_aliases={7: 0} if before else {},
            compiler_params=PARAMS,
            cost_estimate=pl.CostEstimate(flops=10**9, bytes_accessed=6 * 10**6, transcendentals=0),
            name="far",
        )(place, near, states, far_tab, qt, far_factor, gain, *before)
    return out


def solution(mesh):
    return jax.shard_map(
        on_device,
        mesh=mesh,
        in_specs=(
            P(("grp", "seq"), None),
            P(("grp", "seq"), None),
            P(("grp", "seq"), None),
            P(None, ("grp", "seq")),
            P(None, None, ("grp", "seq")),
            P(),
            P(),
        ),
        out_specs=P(("grp", "seq"), None),
        check_vma=False,
    )
```

```python
import functools

import jax
import jax.numpy as jnp
from jax import lax
from jax.experimental import pallas as pl
from jax.experimental.pallas import tpu as pltpu
from jax.sharding import PartitionSpec as P


EPSILON = 1e-05
TILE = 128
GROUP = 16
NEAR_CALLS = (4, 6, 6)
STEP = 2


def log2(value):
    return value.bit_length() - 1


def shape_of(shape, dtype):
    return jax.ShapeDtypeStruct(shape, dtype)


RESIDENT = pl.BlockSpec(memory_space=pltpu.VMEM)
PARAMS = pltpu.CompilerParams(vmem_limit_bytes=24 << 20)


def rows_of(head, width):
    return pl.ds(pl.multiple_of(head * width, width), width)


def tile_decays(log_decay):
    length = log_decay.shape[1]
    row = lax.broadcasted_iota(jnp.int32, (TILE, TILE), 0)
    col = lax.broadcasted_iota(jnp.int32, (TILE, TILE), 1)
    parts = [log_decay[:, at : at + TILE] for at in range(0, length, TILE)]
    local = lax.dot_general(
        jnp.concatenate(parts, axis=0),
        (row <= col).astype(jnp.float32),
        (((1,), (0,)), ((), ())),
        precision=lax.Precision.HIGHEST,
        preferred_element_type=jnp.float32,
    )
    middle = jnp.broadcast_to(local[:, TILE // 2 - 1 : TILE // 2], local.shape)
    total = jnp.broadcast_to(local[:, TILE - 1 : TILE], local.shape)
    heads = log_decay.shape[0]

    def split(array):
        return [array[at : at + heads] for at in range(0, array.shape[0], heads)]

    return split(local), split(middle), split(total)


def pair_row(table, head, pair):
    sides = [table[2 * pair + side, pl.ds(head, 1), :] for side in range(2)]
    return jnp.concatenate(sides, axis=1)


def conv_tile(buf, weight, start):
    taps = weight.shape[0]
    total = None
    for tap in range(taps):
        term = weight[tap : tap + 1, :] * buf[pl.ds(8 - (taps - 1) + tap + start, TILE), :]
        total = term if total is None else total + term
    return total + total * jnp.tanh(total)


def fill(buf, source, rim):
    length = source.shape[0]
    buf[pl.ds(8 - rim.shape[0], rim.shape[0]), :] = rim[...].astype(jnp.float32)
    buf[pl.ds(8, length), :] = source[...].astype(jnp.float32)


def state_keys(pairs):
    return [
        (bit, first)
        for bit in range(log2(pairs))
        for first in range(0, pairs, 2 << bit)
    ]


def three_terms(wide):
    terms = []
    for _ in range(3):
        term = wide.astype(jnp.bfloat16)
        terms.append(term)
        wide = wide - term.astype(jnp.float32)
    terms.append(jnp.zeros_like(terms[0]))
    return jnp.concatenate(terms, axis=0)


def sum_terms(terms):
    each = terms.shape[0] // 4
    wide = terms.astype(jnp.float32)
    return wide[:each] + wide[each : 2 * each] + wide[2 * each : 3 * each]


def state_kernel(
    k_ref, v_ref, rim_ref, wk_ref, wv_ref, ld_ref,
    vt_ref, st_ref, g_ref, kc_ref,
    buf, scale, total, values, sems,
):
    step = pl.program_id(0)
    heads = ld_ref.shape[0]
    length = v_ref.shape[0]
    width = v_ref.shape[1] // heads
    state_dim = k_ref.shape[1]
    pairs = length // (2 * TILE)
    steps = heads // STEP

    def fetch(order):
        lanes = slice(order * STEP * width, (order + 1) * STEP * width)
        return pltpu.make_async_copy(v_ref.at[:, lanes], values.at[order], sems.at[order])

    @pl.when(step == 0)
    def _():
        for order in range(steps):
            fetch(order).start()
        local, _, totals = tile_decays(ld_ref[...])
        summed = None
        for pair in range(pairs):
            low, high = 2 * pair, 2 * pair + 1
            scale[low] = jnp.exp(totals[low] - local[low] + totals[high])
            scale[high] = jnp.exp(totals[high] - local[high])
            both = totals[low] + totals[high]
            total[pair] = jnp.exp(both)
            summed = both if summed is None else summed + both
        g_ref[pl.ds(heads * width, 4 * heads), :] = three_terms(summed)
        fill(buf.at[0], k_ref, rim_ref.at[:, state_dim : 2 * state_dim])
        for tile in range(length // TILE):
            at = tile * TILE
            kc_ref[at : at + TILE, :] = conv_tile(buf.at[0], 0.5 * wk_ref[...], at).astype(jnp.bfloat16)

    for order in range(steps):

        @pl.when(step == order)
        def _(order=order):
            fetch(order).wait()

    for place in range(STEP):
        lanes = slice(place * width, (place + 1) * width)
        rim_lanes = pl.ds(pl.multiple_of(2 * state_dim + (step * STEP + place) * width, width), width)
        fill(buf.at[place], values.at[step, :, lanes], rim_ref.at[:, rim_lanes])
    for place in range(STEP):
        head = step * STEP + place
        lanes = slice(place * width, (place + 1) * width)
        weight = 0.5 * wv_ref[:, lanes]
        states = {}
        for pair in range(pairs):
            at = 2 * pair * TILE
            sides = []
            for start in (at, at + TILE):
                done = conv_tile(buf.at[place], weight, start).astype(jnp.bfloat16).T
                vt_ref[rows_of(head, width), start : start + TILE] = done
                sides.append(done)
            row = pair_row(scale, head, pair).astype(jnp.bfloat16)
            states[(0, pair)] = jnp.dot(
                jnp.concatenate(sides, axis=1) * row,
                kc_ref[at : at + 2 * TILE, :],
                preferred_element_type=jnp.float32,
            )
        decay = [total[pair, pl.ds(head, 1), :] for pair in range(pairs)]
        for bit in range(log2(pairs)):
            for first in range(0, pairs, 2 << bit):
                keep = states[(bit, first + (1 << bit))]
                factor = decay[first + (1 << bit)]
                for later in range(first + (1 << bit) + 1, first + (2 << bit)):
                    factor = factor * decay[later]
                states[(bit + 1, first)] = keep + factor * states[(bit, first)]
        for order, key in enumerate(state_keys(pairs)):
            st_ref[order, rows_of(head, width), :] = states[key].astype(jnp.bfloat16)
        g_ref[rows_of(head, width), :] = states[(log2(pairs), 0)].astype(jnp.bfloat16)


def table_rows(length):
    inner = log2(GROUP) + 1
    groups = TILE // GROUP
    states = log2(length // (2 * TILE))
    return {
        "inner": 0,
        "group": inner,
        "sibling": inner + groups,
        "value": inner + groups + 1,
        "state": inner + groups + 2,
        "size": inner + groups + 2 + states,
    }


def table_kernel(ld_ref, lw_ref, tab_ref, far_ref, place_ref):
    index = lax.axis_index("seq")
    place_ref[0] = index & 1
    place_ref[1] = index >> 1 & 1
    place_ref[2] = index >> 2
    heads, length = ld_ref.shape
    levels = lw_ref.shape[0]
    pairs = length // (2 * TILE)
    rows = table_rows(length)
    inner = log2(GROUP) + 1
    tile_level = log2(TILE)
    locals_, middles, totals = tile_decays(ld_ref[...])
    block = lax.broadcasted_iota(jnp.int32, (heads, TILE), 1) // GROUP
    zero = jnp.zeros((heads, TILE), jnp.float32)
    pair_total = []
    running = zero
    for pair in range(pairs):
        low = 2 * pair
        for tile in (low, low + 1):
            lanes = pl.ds(tile * TILE, TILE)
            weight = [lw_ref[level, :, lanes].astype(jnp.float32) for level in range(levels)]
            local = locals_[tile]
            gap = jnp.exp(local - middles[tile])
            scaled = [weight[level] * gap for level in range(tile_level + 1)]
            for level in range(inner):
                tab_ref[rows["inner"] + level, tile] = scaled[level]
            for group in range(TILE // GROUP):
                base = zero
                differ = block ^ group
                for level in range(inner, tile_level + 1):
                    least = 1 << (level - inner)
                    here = (differ >= least) & (differ < 2 * least) & (block > group)
                    base = jnp.where(here, scaled[level], base)
                tab_ref[rows["group"] + group, tile] = base
            tab_ref[rows["value"], tile] = jnp.exp(middles[tile] - local)
            if tile == low:
                tab_ref[rows["sibling"], tile] = zero
            else:
                tab_ref[rows["sibling"], tile] = weight[tile_level + 1] * jnp.exp(
                    local + totals[low] - middles[low]
                )
                local = local + totals[low]
            for bit in range(log2(pairs)):
                since = zero
                for other in range(pair >> bit << bit, pair):
                    since = since + pair_total[other]
                tab_ref[rows["state"] + bit, tile] = weight[tile_level + 2 + bit] * jnp.exp(
                    local + since
                )
            whole_decay = jnp.exp(local + running)
            first = log2(length) + 1
            for level in range(first, levels):
                far_ref[level - first, tile] = weight[level] * whole_decay
        pair_total.append(totals[low] + totals[low + 1])
        running = running + pair_total[-1]


def rim_kernel(q_ref, k_ref, v_ref, out_ref, last, sems):
    rows, state_dim = out_ref.shape[0], q_ref.shape[1]
    tail = pl.ds(q_ref.shape[0] - GROUP, GROUP)
    lanes = (
        slice(0, state_dim),
        slice(state_dim, 2 * state_dim),
        slice(2 * state_dim, 2 * state_dim + v_ref.shape[1]),
    )
    copies = [
        pltpu.make_async_copy(ref.at[tail, :], last.at[:, at], sems.at[order])
        for order, (ref, at) in enumerate(zip((q_ref, k_ref, v_ref), lanes, strict=True))
    ]
    for copy in copies:
        copy.start()
    for copy in copies:
        copy.wait()
    out_ref[...] = last[GROUP - rows :, :]


def score_kernel(q_ref, rim_ref, w_ref, kc_ref, qt_ref, sc_ref, buf):
    length, state_dim = q_ref.shape
    fill(buf, q_ref, rim_ref.at[:, 0:state_dim])
    weight = 0.5 * w_ref[:, 0:state_dim]
    for at in range(0, length, TILE):
        qt_ref[:, at : at + TILE] = conv_tile(buf, weight, at).astype(jnp.bfloat16).T
    for pair in range(sc_ref.shape[0]):
        at = 2 * pair * TILE
        sc_ref[pair] = jnp.dot(
            kc_ref[at : at + 2 * TILE, :],
            qt_ref[:, at : at + 2 * TILE],
            preferred_element_type=jnp.float32,
        ).astype(jnp.bfloat16)


def near_kernel(first_head, width, vt_ref, st_ref, tab_ref, sc, qt_ref, near_ref, mix, rest):
    length = vt_ref.shape[1]
    pairs = length // (2 * TILE)
    rows = table_rows(length)
    inner = log2(GROUP) + 1
    row = lax.broadcasted_iota(jnp.int32, (GROUP, TILE), 0)
    lane = lax.broadcasted_iota(jnp.int32, (GROUP, TILE), 1)
    within = lane % GROUP
    differ = row ^ within
    keys = state_keys(pairs)

    @pl.when(pl.program_id(0) == 0)
    def _():
        for pair in range(pairs):
            for place in range(STEP):
                mix[place, pair, TILE:, 0:TILE] = jnp.zeros((TILE, TILE), jnp.bfloat16)

    def one_head(place):
        head = first_head + pl.program_id(0) * STEP + place
        own = rows_of(head, width)

        def table(order, tile):
            return tab_ref[order, tile, pl.ds(head, 1), :]

        for pair in range(pairs):
            at = 2 * pair * TILE
            for side in range(2):
                tile = 2 * pair + side
                diagonal = jnp.where(differ == 0, table(rows["inner"], tile), 0.0)
                for level in range(1, inner):
                    here = (differ >= 1 << (level - 1)) & (differ < 1 << level) & (row < within)
                    diagonal = jnp.where(here, table(rows["inner"] + level, tile), diagonal)
                lanes = slice(side * TILE, (side + 1) * TILE)
                for group in range(TILE // GROUP):
                    base = table(rows["group"] + group, tile)
                    weight = jnp.where(lane // GROUP == group, diagonal, base).astype(jnp.bfloat16)
                    start = side * TILE + group * GROUP
                    mix[place, pair, start : start + GROUP, lanes] = (
                        sc[pair, start : start + GROUP, lanes] * weight
                    )
            mix[place, pair, 0:TILE, TILE:] = sc[pair, 0:TILE, TILE:] * table(
                rows["sibling"], 2 * pair + 1
            ).astype(jnp.bfloat16)
            value = vt_ref[own, at : at + 2 * TILE] * pair_row(
                tab_ref.at[rows["value"]], head, pair
            ).astype(jnp.bfloat16)
            summed = jnp.dot(value, mix[place, pair], preferred_element_type=jnp.float32)
            active = [bit for bit in range(log2(pairs)) if pair >> bit & 1]
            if active:
                held = []
                for order, bit in enumerate(active):
                    scale = pair_row(tab_ref.at[rows["state"] + bit], head, pair).astype(jnp.bfloat16)
                    rest[place, pair, order * TILE : (order + 1) * TILE, :] = (
                        qt_ref[:, at : at + 2 * TILE] * scale
                    )
                    held.append(st_ref[keys.index((bit, pair >> bit + 1 << bit + 1)), own, :])
                summed = summed + jnp.dot(
                    jnp.concatenate(held, axis=1),
                    rest[place, pair, 0 : len(active) * TILE, :],
                    preferred_element_type=jnp.float32,
                )
            near_ref[own, at : at + 2 * TILE] = summed.astype(jnp.bfloat16)

    for place in range(STEP):
        one_head(place)


def add_far(levels, head, width, near_ref, buckets, far_ref, qt_ref, off_ref, rest, finish):
    length = qt_ref.shape[1]
    held = jnp.concatenate(buckets, axis=1)
    factors = []
    for level in levels:
        factor = off_ref[level, pl.ds(head, 1), :]
        factors.append(jnp.concatenate([factor, factor], axis=1))
    for pair in range(length // (2 * TILE)):
        at = 2 * pair * TILE
        for order, level in enumerate(levels):
            row = (pair_row(far_ref.at[level], head, pair) * factors[order]).astype(jnp.bfloat16)
            rest[pair, order * TILE : (order + 1) * TILE, :] = qt_ref[:, at : at + 2 * TILE] * row
        summed = near_ref[rows_of(head, width), at : at + 2 * TILE].astype(jnp.float32) + jnp.dot(
            held, rest[pair], preferred_element_type=jnp.float32
        )
        finish(at, summed)


def mid_kernel(
    width, place_ref, near_ref, chip_ref, low_ref, low_other_ref, far_ref, qt_ref, off_ref, out_ref, rest
):
    step, steps = pl.program_id(0), pl.num_programs(0)
    for place in range(STEP):
        own = slice(place * width, (place + 1) * width)
        head = lax.rem(place_ref[0] * (steps // 2) + step, steps) * STEP + place
        low = jnp.where(step < steps // 2, low_ref[own, :], low_other_ref[own, :])

        def finish(at, summed, head=head):
            out_ref[rows_of(head, width), at : at + 2 * TILE] = summed.astype(jnp.bfloat16)

        add_far(
            (0, 1), head, width, near_ref, [chip_ref[own, :], low], far_ref, qt_ref, off_ref, rest.at[place], finish
        )


def far_kernel(width, other, place_ref, near_ref, high_ref, far_ref, qt_ref, off_ref, gain_ref, *refs):
    out_ref, rest = refs[-2:]
    count = high_ref.shape[0]
    for place in range(STEP):
        own = slice(place * width, (place + 1) * width)
        core = 1 - place_ref[0] if other else place_ref[0]
        head = (core * pl.num_programs(0) + pl.program_id(0)) * STEP + place
        gain = jnp.broadcast_to(gain_ref[:, own], (TILE, TILE)).T

        def finish(at, summed, own=own, gain=gain):
            mean = jnp.mean(summed * summed, axis=0, keepdims=True)
            normed = summed * lax.rsqrt(mean + EPSILON)
            for side in range(2):
                part = normed[:, side * TILE : (side + 1) * TILE] * gain
                start = at + side * TILE
                out_ref[start : start + TILE, own] = part.astype(jnp.bfloat16).T

        add_far(
            tuple(range(2, 2 + count)),
            head,
            width,
            near_ref,
            [high_ref[level, own, :] for level in range(count)],
            far_ref,
            qt_ref,
            off_ref,
            rest.at[place],
            finish,
        )


def core_kernel(width, place_ref, own_ref, other_ref, theirs_ref, mine_ref, keep_ref, factor):
    heads = keep_ref.shape[1]
    states = heads * width
    quarter = heads // 4
    core, side = place_ref[0], place_ref[1]
    upper = core == 1
    own_total = sum_terms(own_ref[states:, :])
    other_total = sum_terms(other_ref[states:, :])
    factor[...] = jnp.exp(jnp.where(upper, own_total, other_total))
    keep_ref[0] = own_total + other_total
    keep_ref[1] = jnp.where(upper, other_total, 0.0)
    for out_ref, column in ((theirs_ref, 1 - side), (mine_ref, side)):
        for order in range(quarter):
            head = (core * 2 + column) * quarter + order
            own = own_ref[rows_of(head, width), :].astype(jnp.float32)
            other = other_ref[rows_of(head, width), :].astype(jnp.float32)
            scale = factor[pl.ds(head, 1), :]
            last, first = jnp.where(upper, own, other), jnp.where(upper, other, own)
            out_ref[order * width : (order + 1) * width, :] = (last + scale * first).astype(jnp.bfloat16)
    theirs_ref[quarter * width :, :] = three_terms(own_total + other_total)


def side_kernel(width, place_ref, got_ref, mine_ref, chip_ref, message_ref, keep_ref, factor):
    heads = keep_ref.shape[1]
    quarter = heads // 4
    core, side = place_ref[0], place_ref[1]
    upper = side == 1
    chip_total = chip_ref[0]
    got_total = sum_terms(got_ref[quarter * width :, :])
    factor[...] = jnp.exp(jnp.where(upper, chip_total, got_total))
    keep_ref[0] = chip_ref[1]
    keep_ref[1] = chip_ref[1] + jnp.where(upper, got_total, 0.0)
    for order in range(quarter):
        rows = slice(order * width, (order + 1) * width)
        mine, got = mine_ref[rows, :].astype(jnp.float32), got_ref[rows, :].astype(jnp.float32)
        scale = factor[pl.ds((core * 2 + side) * quarter + order, 1), :]
        last, first = jnp.where(upper, mine, got), jnp.where(upper, got, mine)
        message_ref[rows, :] = (last + scale * first).astype(jnp.bfloat16)
    message_ref[quarter * width :, :] = three_terms(chip_total + got_total)


def plane_kernel(width, place_ref, *refs):
    far_ref, part_ref, factor = refs[-3:]
    came, keep_ref = refs[:-4], refs[-4]
    heads = keep_ref.shape[1]
    quarter = heads // 4
    core, side, plane = place_ref[0], place_ref[1], place_ref[2]
    planes = len(came) + 1
    totals = [sum_terms(ref[quarter * width :, :]) for ref in came]
    zero = jnp.zeros_like(totals[0])
    far_ref[0] = jnp.where(core == 1, jnp.ones_like(zero), 0.0)
    far_ref[1] = jnp.where(side == 1, jnp.exp(keep_ref[0]), 0.0)
    in_plane = jnp.exp(keep_ref[1])
    for bit in range(log2(planes)):
        upper = (plane >> bit) & 1 == 1
        far_ref[2 + bit] = jnp.where(upper, in_plane, 0.0)
        if bit == 0:
            continue
        for by in range(1, planes):
            source = plane ^ by
            here = upper & (source >> (bit + 1) == plane >> (bit + 1)) & ((source >> bit) & 1 == 0)
            between = zero
            for mid in range(1, planes):
                inside = (plane ^ mid > source) & (plane ^ mid < plane)
                between = between + jnp.where(inside, totals[mid - 1], 0.0)
            factor[by - 1] = jnp.where(here, jnp.exp(between), 0.0)
        for order in range(quarter):
            rows = slice(order * width, (order + 1) * width)
            head = (core * 2 + side) * quarter + order
            summed = None
            for by in range(1, planes):
                term = factor[by - 1, pl.ds(head, 1), :] * came[by - 1][rows, :].astype(jnp.float32)
                summed = term if summed is None else summed + term
            part_ref[bit - 1, rows, :] = summed.astype(jnp.bfloat16)


def stack_kernel(first_ref, last_ref, out_ref):
    half = first_ref.shape[0]
    out_ref[0:half, :] = first_ref[...]
    out_ref[half:, :] = last_ref[0:half, :]


def column_kernel(place_ref, next_ref, next_swapped_ref, part_ref, swapped_ref, out_ref):
    side = place_ref[1]
    count, quarter, _ = part_ref.shape
    mine, theirs = rows_of(side, quarter), rows_of(1 - side, quarter)
    out_ref[0, mine, :] = next_ref[0:quarter, :]
    out_ref[0, theirs, :] = next_swapped_ref[0:quarter, :]
    for level in range(count):
        out_ref[level + 1, mine, :] = part_ref[level]
        out_ref[level + 1, theirs, :] = swapped_ref[level]


def glue(kernel, out_shape, scratch=()):
    scalar = pl.BlockSpec(memory_space=pltpu.SMEM)

    def call(*args, place=None):
        first = [] if place is None else [place]
        many = isinstance(out_shape, list)
        return pl.pallas_call(
            kernel,
            in_specs=[scalar for _ in first] + [RESIDENT for _ in args],
            out_specs=[RESIDENT for _ in out_shape] if many else RESIDENT,
            out_shape=out_shape,
            scratch_shapes=list(scratch),
            compiler_params=PARAMS,
            cost_estimate=pl.CostEstimate(flops=10**7, bytes_accessed=10**6, transcendentals=0),
        )(*first, *args)

    return call


def send(x, by, size):
    return lax.ppermute(x, "seq", [(i, i ^ by) for i in range(size)])


def shift(x, by, size):
    return lax.ppermute(x, "seq", [(i, i + by) for i in range(size - by)])


def on_device(
    query_inputs, key_inputs, value_inputs, log_decay, level_weight, conv_weight, norm_gain
):
    length, state_dim = query_inputs.shape
    heads = log_decay.shape[0]
    values_dim = value_inputs.shape[1]
    width = values_dim // heads
    taps = conv_weight.shape[0]
    rim = taps - 1
    size = lax.axis_size("seq")
    bits = log2(size)
    pairs = length // (2 * TILE)
    keys = state_keys(pairs)
    half, quarter = values_dim // 2, values_dim // 4
    half_heads = heads // 2
    tail = 4 * heads
    half_steps = half_heads // STEP
    gain = norm_gain.reshape(1, values_dim)
    planes = size // 4
    rows = table_rows(length)
    value_inputs = pltpu.with_memory_space_constraint(value_inputs, pltpu.HBM)
    calls = NEAR_CALLS if sum(NEAR_CALLS) == heads else (heads,)

    rim_width = 2 * state_dim + values_dim
    own_rim = pl.pallas_call(
        rim_kernel,
        in_specs=[pl.BlockSpec(memory_space=pltpu.HBM)] * 3,
        out_specs=RESIDENT,
        out_shape=pltpu.VMEM((rim, rim_width), jnp.bfloat16),
        scratch_shapes=[
            pltpu.VMEM((GROUP, rim_width), jnp.bfloat16),
            pltpu.SemaphoreType.DMA((3,)),
        ],
        compiler_params=pltpu.CompilerParams(vmem_limit_bytes=62 << 20),
        name="rim",
    )(query_inputs, key_inputs, value_inputs)
    rims = shift(own_rim, 1, size)

    tab, far_tab, place = pl.pallas_call(
        table_kernel,
        in_specs=[RESIDENT] * 2,
        out_specs=[RESIDENT] * 2 + [pl.BlockSpec(memory_space=pltpu.SMEM)],
        out_shape=[
            pltpu.VMEM((rows["size"], length // TILE, heads, TILE), jnp.float32),
            pltpu.VMEM((bits, length // TILE, heads, TILE), jnp.float32),
            shape_of((3,), jnp.int32),
        ],
        compiler_params=PARAMS,
        cost_estimate=pl.CostEstimate(flops=10**9, bytes_accessed=3 * 10**6, transcendentals=0),
        name="tables",
    )(log_decay, level_weight)

    vt, st, group, kc = pl.pallas_call(
        state_kernel,
        grid=(heads // STEP,),
        in_specs=[
            RESIDENT,
            pl.BlockSpec(memory_space=pl.ANY),
            RESIDENT,
            pl.BlockSpec((taps, state_dim), lambda i: (0, 1)),
            pl.BlockSpec((taps, STEP * width), lambda i: (0, 2 * state_dim // (STEP * width) + i)),
            RESIDENT,
        ],
        out_specs=[RESIDENT] * 4,
        out_shape=[
            pltpu.VMEM((values_dim, length), jnp.bfloat16),
            pltpu.VMEM((len(keys), values_dim, state_dim), jnp.bfloat16),
            pltpu.VMEM((values_dim + tail, state_dim), jnp.bfloat16),
            pltpu.VMEM((length, state_dim), jnp.bfloat16),
        ],
        scratch_shapes=[
            pltpu.VMEM((STEP, length + 8, TILE), jnp.float32),
            pltpu.VMEM((length // TILE, heads, TILE), jnp.float32),
            pltpu.VMEM((pairs, heads, TILE), jnp.float32),
            pltpu.VMEM((heads // STEP, length, STEP * width), jnp.bfloat16),
            pltpu.SemaphoreType.DMA((heads // STEP,)),
        ],
        compiler_params=PARAMS,
        cost_estimate=pl.CostEstimate(flops=10**9, bytes_accessed=9 * 10**6, transcendentals=0),
        name="state",
    )(key_inputs, value_inputs, rims, conv_weight, conv_weight, log_decay)

    qt, sc = pl.pallas_call(
        score_kernel,
        in_specs=[RESIDENT] * 4,
        out_specs=[RESIDENT] * 2,
        out_shape=[
            pltpu.VMEM((state_dim, length), jnp.bfloat16),
            pltpu.VMEM((pairs, 2 * TILE, 2 * TILE), jnp.bfloat16),
        ],
        scratch_shapes=[pltpu.VMEM((length + 8, TILE), jnp.float32)],
        compiler_params=PARAMS,
        cost_estimate=pl.CostEstimate(flops=10**8, bytes_accessed=10**6, transcendentals=0),
        name="scores",
    )(query_inputs, rims, conv_weight, kc)

    near = vt
    for call, each in enumerate(calls):
        near = pl.pallas_call(
            functools.partial(near_kernel, sum(calls[:call]), width),
            grid=(each // STEP,),
            in_specs=[RESIDENT] * 5,
            out_specs=RESIDENT,
            out_shape=pltpu.VMEM((values_dim, length), jnp.bfloat16),
            scratch_shapes=[
                pltpu.VMEM((STEP, pairs, 2 * TILE, 2 * TILE), jnp.bfloat16),
                pltpu.VMEM((STEP, pairs, log2(pairs) * state_dim, 2 * TILE), jnp.bfloat16),
            ],
            input_output_aliases={0: 0},
            compiler_params=PARAMS,
            cost_estimate=pl.CostEstimate(flops=10**9, bytes_accessed=4 * 10**6, transcendentals=0),
            name="near",
        )(near, st, tab, sc, qt)

    other = send(group, 1, size)
    table = pltpu.VMEM((heads, state_dim), jnp.float32)
    message_shape = pltpu.VMEM((quarter + tail, state_dim), jnp.bfloat16)
    theirs, mine, keep = glue(
        functools.partial(core_kernel, width),
        [message_shape, pltpu.VMEM((quarter, state_dim), jnp.bfloat16), pltpu.VMEM((2, heads, state_dim), jnp.float32)],
        [table],
    )(group, other, place=place)

    got = send(theirs, 2, size)
    got_rest = send(mine, 2, size)
    message, keep = glue(
        functools.partial(side_kernel, width), [message_shape, pltpu.VMEM((2, heads, state_dim), jnp.float32)], [table]
    )(got, mine, keep, place=place)

    came = []
    for by in range(1, planes):
        came.append(send(message, 4 * by, size))

    next_swapped = send(came[0], 2, size)

    low = glue(stack_kernel, pltpu.VMEM((half, state_dim), jnp.bfloat16))(got_rest, got)
    low_other = send(low, 1, size)

    count = bits - 2
    far_factor, part = glue(
        functools.partial(plane_kernel, width),
        [pltpu.VMEM((bits, heads, state_dim), jnp.float32), pltpu.VMEM((count - 1, quarter, state_dim), jnp.bfloat16)],
        [pltpu.VMEM((planes - 1, heads, state_dim), jnp.float32)],
    )(*came, keep, place=place)

    near = pl.pallas_call(
        functools.partial(mid_kernel, width),
        grid_spec=pltpu.PrefetchScalarGridSpec(
            num_scalar_prefetch=1,
            grid=(2 * half_steps,),
            in_specs=[
                RESIDENT,
                pl.BlockSpec((STEP * width, state_dim), lambda i, s: (lax.rem(s[0] * half_steps + i, 2 * half_steps), 0)),
                pl.BlockSpec((STEP * width, state_dim), lambda i, s: (jnp.minimum(i, half_steps - 1), 0)),
                pl.BlockSpec((STEP * width, state_dim), lambda i, s: (jnp.maximum(i - half_steps, 0), 0)),
                RESIDENT,
                RESIDENT,
                RESIDENT,
            ],
            out_specs=RESIDENT,
            scratch_shapes=[pltpu.VMEM((STEP, pairs, 2 * state_dim, 2 * TILE), jnp.bfloat16)],
        ),
        out_shape=pltpu.VMEM((values_dim, length), jnp.bfloat16),
        input_output_aliases={1: 0},
        compiler_params=PARAMS,
        cost_estimate=pl.CostEstimate(flops=10**9, bytes_accessed=6 * 10**6, transcendentals=0),
        name="mid",
    )(place, near, other, low, low_other, far_tab, qt, far_factor)

    swapped = send(part, 2, size)
    high = glue(column_kernel, pltpu.VMEM((count, half, state_dim), jnp.bfloat16))(
        came[0], next_swapped, part, swapped, place=place
    )
    high_other = send(high, 1, size)

    out = None
    for call, states in enumerate((high, high_other)):
        before = [] if out is None else [out]

        def columns(i, s, other=call):
            return (0, (1 - s[0] if other else s[0]) * half_steps + i)

        out = pl.pallas_call(
            functools.partial(far_kernel, width, call),
            grid_spec=pltpu.PrefetchScalarGridSpec(
                num_scalar_prefetch=1,
                grid=(half_steps,),
                in_specs=[
                    RESIDENT,
                    pl.BlockSpec((count, STEP * width, state_dim), lambda i, s: (0, i, 0)),
                    RESIDENT,
                    RESIDENT,
                    RESIDENT,
                    pl.BlockSpec((1, STEP * width), columns),
                ]
                + [pl.BlockSpec(memory_space=pl.ANY) for _ in before],
                out_specs=pl.BlockSpec((length, STEP * width), columns),
                scratch_shapes=[pltpu.VMEM((STEP, pairs, count * state_dim, 2 * TILE), jnp.bfloat16)],
            ),
            out_shape=shape_of((length, values_dim), jnp.bfloat16),
            input_output_aliases={7: 0} if before else {},
            compiler_params=PARAMS,
            cost_estimate=pl.CostEstimate(flops=10**9, bytes_accessed=6 * 10**6, transcendentals=0),
            name="far",
        )(place, near, states, far_tab, qt, far_factor, gain, *before)
    return out


def solution(mesh):
    return jax.shard_map(
        on_device,
        mesh=mesh,
        in_specs=(
            P(("grp", "seq"), None),
            P(("grp", "seq"), None),
            P(("grp", "seq"), None),
            P(None, ("grp", "seq")),
            P(None, None, ("grp", "seq")),
            P(),
            P(),
        ),
        out_specs=P(("grp", "seq"), None),
        check_vma=False,
    )
```

```python
import functools

import jax
import jax.numpy as jnp
from jax import lax
from jax.experimental import pallas as pl
from jax.experimental.pallas import tpu as pltpu
from jax.sharding import PartitionSpec as P


EPSILON = 1e-05
TILE = 128
GROUP = 16
NEAR_CALLS = (6, 4, 6)
STEP = 2


def log2(value):
    return value.bit_length() - 1


def shape_of(shape, dtype):
    return jax.ShapeDtypeStruct(shape, dtype)


RESIDENT = pl.BlockSpec(memory_space=pltpu.VMEM)
PARAMS = pltpu.CompilerParams(vmem_limit_bytes=24 << 20)


def rows_of(head, width):
    return pl.ds(pl.multiple_of(head * width, width), width)


def tile_decays(log_decay):
    length = log_decay.shape[1]
    row = lax.broadcasted_iota(jnp.int32, (TILE, TILE), 0)
    col = lax.broadcasted_iota(jnp.int32, (TILE, TILE), 1)
    parts = [log_decay[:, at : at + TILE] for at in range(0, length, TILE)]
    local = lax.dot_general(
        jnp.concatenate(parts, axis=0),
        (row <= col).astype(jnp.float32),
        (((1,), (0,)), ((), ())),
        precision=lax.Precision.HIGHEST,
        preferred_element_type=jnp.float32,
    )
    middle = jnp.broadcast_to(local[:, TILE // 2 - 1 : TILE // 2], local.shape)
    total = jnp.broadcast_to(local[:, TILE - 1 : TILE], local.shape)
    heads = log_decay.shape[0]

    def split(array):
        return [array[at : at + heads] for at in range(0, array.shape[0], heads)]

    return split(local), split(middle), split(total)


def pair_row(table, head, pair):
    sides = [table[2 * pair + side, pl.ds(head, 1), :] for side in range(2)]
    return jnp.concatenate(sides, axis=1)


def conv_tile(buf, weight, start):
    taps = weight.shape[0]
    total = None
    for tap in range(taps):
        term = weight[tap : tap + 1, :] * buf[pl.ds(8 - (taps - 1) + tap + start, TILE), :]
        total = term if total is None else total + term
    return total + total * jnp.tanh(total)


def fill(buf, source, rim):
    length = source.shape[0]
    buf[pl.ds(8 - rim.shape[0], rim.shape[0]), :] = rim[...].astype(jnp.float32)
    buf[pl.ds(8, length), :] = source[...].astype(jnp.float32)


def state_keys(pairs):
    return [
        (bit, first)
        for bit in range(log2(pairs))
        for first in range(0, pairs, 2 << bit)
    ]


def three_terms(wide):
    lane = lax.broadcasted_iota(jnp.int32, wide.shape, 1)
    terms = jnp.zeros_like(wide)
    for order in range(3):
        term = wide.astype(jnp.bfloat16).astype(jnp.float32)
        terms = jnp.where(lane == order, term, terms)
        wide = wide - term
    return terms.astype(jnp.bfloat16)


def sum_terms(terms):
    wide = terms.astype(jnp.float32)
    return jnp.broadcast_to(wide[:, 0:1] + wide[:, 1:2] + wide[:, 2:3], wide.shape)


def state_kernel(
    k_ref, v_ref, rim_ref, wk_ref, wv_ref, ld_ref,
    vt_ref, st_ref, g_ref, kc_ref,
    buf, scale, total, values, sems,
):
    step = pl.program_id(0)
    heads = ld_ref.shape[0]
    length = v_ref.shape[0]
    width = v_ref.shape[1] // heads
    state_dim = k_ref.shape[1]
    pairs = length // (2 * TILE)
    steps = heads // STEP

    def fetch(order):
        lanes = slice(order * STEP * width, (order + 1) * STEP * width)
        return pltpu.make_async_copy(v_ref.at[:, lanes], values.at[order], sems.at[order])

    @pl.when(step == 0)
    def _():
        for order in range(steps):
            fetch(order).start()
        local, _, totals = tile_decays(ld_ref[...])
        summed = None
        for pair in range(pairs):
            low, high = 2 * pair, 2 * pair + 1
            scale[low] = jnp.exp(totals[low] - local[low] + totals[high])
            scale[high] = jnp.exp(totals[high] - local[high])
            both = totals[low] + totals[high]
            total[pair] = jnp.exp(both)
            summed = both if summed is None else summed + both
        g_ref[pl.ds(heads * width, heads), :] = three_terms(summed)
        fill(buf.at[0], k_ref, rim_ref.at[:, state_dim : 2 * state_dim])
        for tile in range(length // TILE):
            at = tile * TILE
            kc_ref[at : at + TILE, :] = conv_tile(buf.at[0], 0.5 * wk_ref[...], at).astype(jnp.bfloat16)

    for order in range(steps):

        @pl.when(step == order)
        def _(order=order):
            fetch(order).wait()

    for place in range(STEP):
        lanes = slice(place * width, (place + 1) * width)
        rim_lanes = pl.ds(pl.multiple_of(2 * state_dim + (step * STEP + place) * width, width), width)
        fill(buf.at[place], values.at[step, :, lanes], rim_ref.at[:, rim_lanes])
    for place in range(STEP):
        head = step * STEP + place
        lanes = slice(place * width, (place + 1) * width)
        weight = 0.5 * wv_ref[:, lanes]
        states = {}
        for pair in range(pairs):
            at = 2 * pair * TILE
            sides = []
            for start in (at, at + TILE):
                done = conv_tile(buf.at[place], weight, start).astype(jnp.bfloat16).T
                vt_ref[rows_of(head, width), start : start + TILE] = done
                sides.append(done)
            row = pair_row(scale, head, pair).astype(jnp.bfloat16)
            states[(0, pair)] = jnp.dot(
                jnp.concatenate(sides, axis=1) * row,
                kc_ref[at : at + 2 * TILE, :],
                preferred_element_type=jnp.float32,
            )
        decay = [total[pair, pl.ds(head, 1), :] for pair in range(pairs)]
        for bit in range(log2(pairs)):
            for first in range(0, pairs, 2 << bit):
                keep = states[(bit, first + (1 << bit))]
                factor = decay[first + (1 << bit)]
                for later in range(first + (1 << bit) + 1, first + (2 << bit)):
                    factor = factor * decay[later]
                states[(bit + 1, first)] = keep + factor * states[(bit, first)]
        for order, key in enumerate(state_keys(pairs)):
            st_ref[order, rows_of(head, width), :] = states[key].astype(jnp.bfloat16)
        g_ref[rows_of(head, width), :] = states[(log2(pairs), 0)].astype(jnp.bfloat16)


def table_rows(length):
    inner = log2(GROUP) + 1
    groups = TILE // GROUP
    states = log2(length // (2 * TILE))
    return {
        "inner": 0,
        "group": inner,
        "sibling": inner + groups,
        "value": inner + groups + 1,
        "state": inner + groups + 2,
        "size": inner + groups + 2 + states,
    }


def table_kernel(ld_ref, lw_ref, tab_ref, far_ref, place_ref):
    index = lax.axis_index("seq")
    place_ref[0] = index & 1
    place_ref[1] = index >> 1 & 1
    place_ref[2] = index >> 2
    heads, length = ld_ref.shape
    levels = lw_ref.shape[0]
    pairs = length // (2 * TILE)
    rows = table_rows(length)
    inner = log2(GROUP) + 1
    tile_level = log2(TILE)
    locals_, middles, totals = tile_decays(ld_ref[...])
    block = lax.broadcasted_iota(jnp.int32, (heads, TILE), 1) // GROUP
    zero = jnp.zeros((heads, TILE), jnp.float32)
    pair_total = []
    running = zero
    for pair in range(pairs):
        low = 2 * pair
        for tile in (low, low + 1):
            lanes = pl.ds(tile * TILE, TILE)
            weight = [lw_ref[level, :, lanes].astype(jnp.float32) for level in range(levels)]
            local = locals_[tile]
            gap = jnp.exp(local - middles[tile])
            scaled = [weight[level] * gap for level in range(tile_level + 1)]
            for level in range(inner):
                tab_ref[rows["inner"] + level, tile] = scaled[level]
            for group in range(TILE // GROUP):
                base = zero
                differ = block ^ group
                for level in range(inner, tile_level + 1):
                    least = 1 << (level - inner)
                    here = (differ >= least) & (differ < 2 * least) & (block > group)
                    base = jnp.where(here, scaled[level], base)
                tab_ref[rows["group"] + group, tile] = base
            tab_ref[rows["value"], tile] = jnp.exp(middles[tile] - local)
            if tile == low:
                tab_ref[rows["sibling"], tile] = zero
            else:
                tab_ref[rows["sibling"], tile] = weight[tile_level + 1] * jnp.exp(
                    local + totals[low] - middles[low]
                )
                local = local + totals[low]
            for bit in range(log2(pairs)):
                since = zero
                for other in range(pair >> bit << bit, pair):
                    since = since + pair_total[other]
                tab_ref[rows["state"] + bit, tile] = weight[tile_level + 2 + bit] * jnp.exp(
                    local + since
                )
            whole_decay = jnp.exp(local + running)
            first = log2(length) + 1
            for level in range(first, levels):
                far_ref[level - first, tile] = weight[level] * whole_decay
        pair_total.append(totals[low] + totals[low + 1])
        running = running + pair_total[-1]


def rim_kernel(q_ref, k_ref, v_ref, out_ref, last, sems):
    rows, state_dim = out_ref.shape[0], q_ref.shape[1]
    tail = pl.ds(q_ref.shape[0] - GROUP, GROUP)
    lanes = (
        slice(0, state_dim),
        slice(state_dim, 2 * state_dim),
        slice(2 * state_dim, 2 * state_dim + v_ref.shape[1]),
    )
    copies = [
        pltpu.make_async_copy(ref.at[tail, :], last.at[:, at], sems.at[order])
        for order, (ref, at) in enumerate(zip((q_ref, k_ref, v_ref), lanes, strict=True))
    ]
    for copy in copies:
        copy.start()
    for copy in copies:
        copy.wait()
    out_ref[...] = last[GROUP - rows :, :]


def score_kernel(q_ref, rim_ref, w_ref, kc_ref, qt_ref, sc_ref, buf):
    length, state_dim = q_ref.shape
    fill(buf, q_ref, rim_ref.at[:, 0:state_dim])
    weight = 0.5 * w_ref[:, 0:state_dim]
    for at in range(0, length, TILE):
        qt_ref[:, at : at + TILE] = conv_tile(buf, weight, at).astype(jnp.bfloat16).T
    for pair in range(sc_ref.shape[0]):
        at = 2 * pair * TILE
        sc_ref[pair] = jnp.dot(
            kc_ref[at : at + 2 * TILE, :],
            qt_ref[:, at : at + 2 * TILE],
            preferred_element_type=jnp.float32,
        ).astype(jnp.bfloat16)


def near_kernel(first_head, width, vt_ref, st_ref, tab_ref, sc, qt_ref, near_ref, mix, rest):
    length = vt_ref.shape[1]
    pairs = length // (2 * TILE)
    rows = table_rows(length)
    inner = log2(GROUP) + 1
    row = lax.broadcasted_iota(jnp.int32, (GROUP, TILE), 0)
    lane = lax.broadcasted_iota(jnp.int32, (GROUP, TILE), 1)
    within = lane % GROUP
    differ = row ^ within
    keys = state_keys(pairs)

    @pl.when(pl.program_id(0) == 0)
    def _():
        for pair in range(pairs):
            for place in range(STEP):
                mix[place, pair, TILE:, 0:TILE] = jnp.zeros((TILE, TILE), jnp.bfloat16)

    def one_head(place):
        head = first_head + pl.program_id(0) * STEP + place
        own = rows_of(head, width)

        def table(order, tile):
            return tab_ref[order, tile, pl.ds(head, 1), :]

        for pair in range(pairs):
            at = 2 * pair * TILE
            for side in range(2):
                tile = 2 * pair + side
                diagonal = jnp.where(differ == 0, table(rows["inner"], tile), 0.0)
                for level in range(1, inner):
                    here = (differ >= 1 << (level - 1)) & (differ < 1 << level) & (row < within)
                    diagonal = jnp.where(here, table(rows["inner"] + level, tile), diagonal)
                lanes = slice(side * TILE, (side + 1) * TILE)
                for group in range(TILE // GROUP):
                    base = table(rows["group"] + group, tile)
                    weight = jnp.where(lane // GROUP == group, diagonal, base).astype(jnp.bfloat16)
                    start = side * TILE + group * GROUP
                    mix[place, pair, start : start + GROUP, lanes] = (
                        sc[pair, start : start + GROUP, lanes] * weight
                    )
            mix[place, pair, 0:TILE, TILE:] = sc[pair, 0:TILE, TILE:] * table(
                rows["sibling"], 2 * pair + 1
            ).astype(jnp.bfloat16)
            value = vt_ref[own, at : at + 2 * TILE] * pair_row(
                tab_ref.at[rows["value"]], head, pair
            ).astype(jnp.bfloat16)
            summed = jnp.dot(value, mix[place, pair], preferred_element_type=jnp.float32)
            active = [bit for bit in range(log2(pairs)) if pair >> bit & 1]
            if active:
                held = []
                for order, bit in enumerate(active):
                    scale = pair_row(tab_ref.at[rows["state"] + bit], head, pair).astype(jnp.bfloat16)
                    rest[place, pair, order * TILE : (order + 1) * TILE, :] = (
                        qt_ref[:, at : at + 2 * TILE] * scale
                    )
                    held.append(st_ref[keys.index((bit, pair >> bit + 1 << bit + 1)), own, :])
                summed = summed + jnp.dot(
                    jnp.concatenate(held, axis=1),
                    rest[place, pair, 0 : len(active) * TILE, :],
                    preferred_element_type=jnp.float32,
                )
            near_ref[own, at : at + 2 * TILE] = summed.astype(jnp.bfloat16)

    for place in range(STEP):
        one_head(place)


def add_far(levels, head, width, near_ref, buckets, far_ref, qt_ref, off_ref, rest, finish):
    length = qt_ref.shape[1]
    held = jnp.concatenate(buckets, axis=1)
    factors = []
    for level in levels:
        factor = off_ref[level, pl.ds(head, 1), :]
        factors.append(jnp.concatenate([factor, factor], axis=1))
    for pair in range(length // (2 * TILE)):
        at = 2 * pair * TILE
        for order, level in enumerate(levels):
            row = (pair_row(far_ref.at[level], head, pair) * factors[order]).astype(jnp.bfloat16)
            rest[pair, order * TILE : (order + 1) * TILE, :] = qt_ref[:, at : at + 2 * TILE] * row
        summed = near_ref[rows_of(head, width), at : at + 2 * TILE].astype(jnp.float32) + jnp.dot(
            held, rest[pair], preferred_element_type=jnp.float32
        )
        finish(at, summed)


def mid_kernel(
    width, near_ref, chip_ref, low_ref, low_other_ref, far_ref, qt_ref, off_ref, out_ref, rest
):
    step, steps = pl.program_id(0), pl.num_programs(0)
    core, _, _ = position()
    half = steps // 2 * STEP
    for place in range(STEP):
        head = lax.rem(core * (steps // 2) + step, steps) * STEP + place
        rows = rows_of(lax.rem(head, half), width)
        low = jnp.where(step < steps // 2, low_ref[rows, :], low_other_ref[rows, :])

        def finish(at, summed, head=head):
            out_ref[rows_of(head, width), at : at + 2 * TILE] = summed.astype(jnp.bfloat16)

        add_far(
            (0, 1), head, width, near_ref, [chip_ref[rows_of(head, width), :], low], far_ref, qt_ref, off_ref, rest.at[place], finish
        )


def far_kernel(width, other, place_ref, near_ref, high_ref, far_ref, qt_ref, off_ref, gain_ref, *refs):
    out_ref, rest = refs[-2:]
    count = high_ref.shape[0]
    for place in range(STEP):
        own = slice(place * width, (place + 1) * width)
        core = 1 - place_ref[0] if other else place_ref[0]
        head = (core * pl.num_programs(0) + pl.program_id(0)) * STEP + place
        gain = jnp.broadcast_to(gain_ref[:, own], (TILE, TILE)).T

        def finish(at, summed, own=own, gain=gain):
            mean = jnp.mean(summed * summed, axis=0, keepdims=True)
            normed = summed * lax.rsqrt(mean + EPSILON)
            for side in range(2):
                part = normed[:, side * TILE : (side + 1) * TILE] * gain
                start = at + side * TILE
                out_ref[start : start + TILE, own] = part.astype(jnp.bfloat16).T

        add_far(
            tuple(range(2, 2 + count)),
            head,
            width,
            near_ref,
            [high_ref[level, own, :] for level in range(count)],
            far_ref,
            qt_ref,
            off_ref,
            rest.at[place],
            finish,
        )


def position():
    index = lax.axis_index("seq")
    return index & 1, index >> 1 & 1, index >> 2


def core_kernel(width, own_ref, other_ref, theirs_ref, mine_ref, keep_ref, factor):
    heads = keep_ref.shape[1]
    states = heads * width
    quarter = heads // 4
    core, side, _ = position()
    upper = core == 1
    own_total = sum_terms(own_ref[states:, :])
    other_total = sum_terms(other_ref[states:, :])
    factor[...] = jnp.exp(jnp.where(upper, own_total, other_total))
    keep_ref[0] = own_total + other_total
    keep_ref[1] = jnp.where(upper, other_total, 0.0)
    for out_ref, column in ((theirs_ref, 1 - side), (mine_ref, side)):
        for order in range(quarter):
            head = (core * 2 + column) * quarter + order
            own = own_ref[rows_of(head, width), :].astype(jnp.float32)
            other = other_ref[rows_of(head, width), :].astype(jnp.float32)
            scale = factor[pl.ds(head, 1), :]
            last, first = jnp.where(upper, own, other), jnp.where(upper, other, own)
            out_ref[order * width : (order + 1) * width, :] = (last + scale * first).astype(jnp.bfloat16)
    theirs_ref[quarter * width :, :] = three_terms(own_total + other_total)


def side_kernel(width, got_ref, mine_ref, chip_ref, message_ref, keep_ref, factor):
    heads = keep_ref.shape[1]
    quarter = heads // 4
    core, side, _ = position()
    upper = side == 1
    chip_total = chip_ref[0]
    got_total = sum_terms(got_ref[quarter * width :, :])
    factor[...] = jnp.exp(jnp.where(upper, chip_total, got_total))
    keep_ref[0] = chip_ref[1]
    keep_ref[1] = chip_ref[1] + jnp.where(upper, got_total, 0.0)
    for order in range(quarter):
        rows = slice(order * width, (order + 1) * width)
        mine, got = mine_ref[rows, :].astype(jnp.float32), got_ref[rows, :].astype(jnp.float32)
        scale = factor[pl.ds((core * 2 + side) * quarter + order, 1), :]
        last, first = jnp.where(upper, mine, got), jnp.where(upper, got, mine)
        message_ref[rows, :] = (last + scale * first).astype(jnp.bfloat16)
    message_ref[quarter * width :, :] = three_terms(chip_total + got_total)


def plane_kernel(width, *refs):
    far_ref, part_ref, factor = refs[-3:]
    came, keep_ref = refs[:-4], refs[-4]
    heads = keep_ref.shape[1]
    quarter = heads // 4
    core, side, plane = position()
    planes = len(came) + 1
    totals = [sum_terms(ref[quarter * width :, :]) for ref in came]
    zero = jnp.zeros_like(totals[0])
    far_ref[0] = jnp.where(core == 1, jnp.ones_like(zero), 0.0)
    far_ref[1] = jnp.where(side == 1, jnp.exp(keep_ref[0]), 0.0)
    in_plane = jnp.exp(keep_ref[1])
    for bit in range(log2(planes)):
        upper = (plane >> bit) & 1 == 1
        far_ref[2 + bit] = jnp.where(upper, in_plane, 0.0)
        if bit == 0:
            continue
        for by in range(1, planes):
            source = plane ^ by
            here = upper & (source >> (bit + 1) == plane >> (bit + 1)) & ((source >> bit) & 1 == 0)
            between = zero
            for mid in range(1, planes):
                inside = (plane ^ mid > source) & (plane ^ mid < plane)
                between = between + jnp.where(inside, totals[mid - 1], 0.0)
            factor[by - 1] = jnp.where(here, jnp.exp(between), 0.0)
        for order in range(quarter):
            rows = slice(order * width, (order + 1) * width)
            head = (core * 2 + side) * quarter + order
            summed = None
            for by in range(1, planes):
                term = factor[by - 1, pl.ds(head, 1), :] * came[by - 1][rows, :].astype(jnp.float32)
                summed = term if summed is None else summed + term
            part_ref[bit - 1, rows, :] = summed.astype(jnp.bfloat16)


def stack_kernel(first_ref, last_ref, out_ref):
    half = first_ref.shape[0]
    out_ref[0:half, :] = first_ref[...]
    out_ref[half:, :] = last_ref[0:half, :]


def column_kernel(next_ref, next_swapped_ref, part_ref, swapped_ref, out_ref):
    _, side, _ = position()
    count, quarter, _ = part_ref.shape
    mine, theirs = rows_of(side, quarter), rows_of(1 - side, quarter)
    out_ref[0, mine, :] = next_ref[0:quarter, :]
    out_ref[0, theirs, :] = next_swapped_ref[0:quarter, :]
    for level in range(count):
        out_ref[level + 1, mine, :] = part_ref[level]
        out_ref[level + 1, theirs, :] = swapped_ref[level]


def glue(kernel, out_shape, scratch=()):
    def call(*args):
        many = isinstance(out_shape, list)
        return pl.pallas_call(
            kernel,
            in_specs=[RESIDENT for _ in args],
            out_specs=[RESIDENT for _ in out_shape] if many else RESIDENT,
            out_shape=out_shape,
            scratch_shapes=list(scratch),
            compiler_params=PARAMS,
            cost_estimate=pl.CostEstimate(flops=10**7, bytes_accessed=10**6, transcendentals=0),
        )(*args)

    return call


def send(x, by, size):
    return lax.ppermute(x, "seq", [(i, i ^ by) for i in range(size)])


def on_device(
    query_inputs, key_inputs, value_inputs, log_decay, level_weight, conv_weight, norm_gain
):
    length, state_dim = query_inputs.shape
    heads = log_decay.shape[0]
    values_dim = value_inputs.shape[1]
    width = values_dim // heads
    taps = conv_weight.shape[0]
    rim = taps - 1
    size = lax.axis_size("seq")
    bits = log2(size)
    pairs = length // (2 * TILE)
    keys = state_keys(pairs)
    half, quarter = values_dim // 2, values_dim // 4
    half_heads = heads // 2
    tail = heads
    half_steps = half_heads // STEP
    gain = norm_gain.reshape(1, values_dim)
    planes = size // 4
    rows = table_rows(length)
    value_inputs = pltpu.with_memory_space_constraint(value_inputs, pltpu.HBM)
    calls = NEAR_CALLS if sum(NEAR_CALLS) == heads else (heads,)

    rim_width = 2 * state_dim + values_dim
    own_rim = pl.pallas_call(
        rim_kernel,
        in_specs=[pl.BlockSpec(memory_space=pltpu.HBM)] * 3,
        out_specs=RESIDENT,
        out_shape=pltpu.VMEM((rim, rim_width), jnp.bfloat16),
        scratch_shapes=[
            pltpu.VMEM((GROUP, rim_width), jnp.bfloat16),
            pltpu.SemaphoreType.DMA((3,)),
        ],
        compiler_params=pltpu.CompilerParams(vmem_limit_bytes=62 << 20),
        name="rim",
    )(query_inputs, key_inputs, value_inputs)
    rims = lax.ppermute(own_rim, "seq", [(i, i + 1) for i in range(size - 1)])

    tab, far_tab, place = pl.pallas_call(
        table_kernel,
        in_specs=[RESIDENT] * 2,
        out_specs=[RESIDENT] * 2 + [pl.BlockSpec(memory_space=pltpu.SMEM)],
        out_shape=[
            pltpu.VMEM((rows["size"], length // TILE, heads, TILE), jnp.float32),
            pltpu.VMEM((bits, length // TILE, heads, TILE), jnp.float32),
            shape_of((3,), jnp.int32),
        ],
        compiler_params=PARAMS,
        cost_estimate=pl.CostEstimate(flops=10**9, bytes_accessed=3 * 10**6, transcendentals=0),
        name="tables",
    )(log_decay, level_weight)

    vt, st, group, kc = pl.pallas_call(
        state_kernel,
        grid=(heads // STEP,),
        in_specs=[
            RESIDENT,
            pl.BlockSpec(memory_space=pl.ANY),
            RESIDENT,
            pl.BlockSpec((taps, state_dim), lambda i: (0, 1)),
            pl.BlockSpec((taps, STEP * width), lambda i: (0, 2 * state_dim // (STEP * width) + i)),
            RESIDENT,
        ],
        out_specs=[RESIDENT] * 4,
        out_shape=[
            pltpu.VMEM((values_dim, length), jnp.bfloat16),
            pltpu.VMEM((len(keys), values_dim, state_dim), jnp.bfloat16),
            pltpu.VMEM((values_dim + tail, state_dim), jnp.bfloat16),
            pltpu.VMEM((length, state_dim), jnp.bfloat16),
        ],
        scratch_shapes=[
            pltpu.VMEM((STEP, length + 8, TILE), jnp.float32),
            pltpu.VMEM((length // TILE, heads, TILE), jnp.float32),
            pltpu.VMEM((pairs, heads, TILE), jnp.float32),
            pltpu.VMEM((heads // STEP, length, STEP * width), jnp.bfloat16),
            pltpu.SemaphoreType.DMA((heads // STEP,)),
        ],
        compiler_params=PARAMS,
        cost_estimate=pl.CostEstimate(flops=10**9, bytes_accessed=9 * 10**6, transcendentals=0),
        name="state",
    )(key_inputs, value_inputs, rims, conv_weight, conv_weight, log_decay)

    qt, sc = pl.pallas_call(
        score_kernel,
        in_specs=[RESIDENT] * 4,
        out_specs=[RESIDENT] * 2,
        out_shape=[
            pltpu.VMEM((state_dim, length), jnp.bfloat16),
            pltpu.VMEM((pairs, 2 * TILE, 2 * TILE), jnp.bfloat16),
        ],
        scratch_shapes=[pltpu.VMEM((length + 8, TILE), jnp.float32)],
        compiler_params=PARAMS,
        cost_estimate=pl.CostEstimate(flops=10**8, bytes_accessed=10**6, transcendentals=0),
        name="scores",
    )(query_inputs, rims, conv_weight, kc)

    near = vt
    for call, each in enumerate(calls):
        near = pl.pallas_call(
            functools.partial(near_kernel, sum(calls[:call]), width),
            grid=(each // STEP,),
            in_specs=[RESIDENT] * 5,
            out_specs=RESIDENT,
            out_shape=pltpu.VMEM((values_dim, length), jnp.bfloat16),
            scratch_shapes=[
                pltpu.VMEM((STEP, pairs, 2 * TILE, 2 * TILE), jnp.bfloat16),
                pltpu.VMEM((STEP, pairs, log2(pairs) * state_dim, 2 * TILE), jnp.bfloat16),
            ],
            input_output_aliases={0: 0},
            compiler_params=PARAMS,
            cost_estimate=pl.CostEstimate(flops=10**9, bytes_accessed=4 * 10**6, transcendentals=0),
            name="near",
        )(near, st, tab, sc, qt)

    other = send(group, 1, size)
    table = pltpu.VMEM((heads, state_dim), jnp.float32)
    message_shape = pltpu.VMEM((quarter + tail, state_dim), jnp.bfloat16)
    theirs, mine, keep = glue(
        functools.partial(core_kernel, width),
        [
            message_shape,
            pltpu.VMEM((quarter, state_dim), jnp.bfloat16),
            pltpu.VMEM((2, heads, state_dim), jnp.float32),
        ],
        [table],
    )(group, other)

    got = send(theirs, 2, size)
    got_rest = send(mine, 2, size)
    message, keep = glue(
        functools.partial(side_kernel, width),
        [message_shape, pltpu.VMEM((2, heads, state_dim), jnp.float32)],
        [table],
    )(got, mine, keep)

    came = []
    for by in range(1, planes):
        came.append(send(message, 4 * by, size))

    next_swapped = send(came[0], 2, size)

    low = glue(stack_kernel, pltpu.VMEM((half, state_dim), jnp.bfloat16))(got_rest, got)
    low_other = send(low, 1, size)

    count = bits - 2
    far_factor, part = glue(
        functools.partial(plane_kernel, width),
        [
            pltpu.VMEM((bits, heads, state_dim), jnp.float32),
            pltpu.VMEM((count - 1, quarter, state_dim), jnp.bfloat16),
        ],
        [pltpu.VMEM((planes - 1, heads, state_dim), jnp.float32)],
    )(*came, keep)

    near = pl.pallas_call(
        functools.partial(mid_kernel, width),
        grid=(2 * half_steps,),
        in_specs=[RESIDENT] * 7,
        out_specs=RESIDENT,
        scratch_shapes=[pltpu.VMEM((STEP, pairs, 2 * state_dim, 2 * TILE), jnp.bfloat16)],
        out_shape=pltpu.VMEM((values_dim, length), jnp.bfloat16),
        input_output_aliases={0: 0},
        compiler_params=PARAMS,
        cost_estimate=pl.CostEstimate(flops=10**9, bytes_accessed=6 * 10**6, transcendentals=0),
        name="mid",
    )(near, other, low, low_other, far_tab, qt, far_factor)

    swapped = send(part, 2, size)
    high = glue(column_kernel, pltpu.VMEM((count, half, state_dim), jnp.bfloat16))(
        came[0], next_swapped, part, swapped
    )
    high_other = send(high, 1, size)

    out = None
    for call, states in enumerate((high, high_other)):
        before = [] if out is None else [out]

        def columns(i, s, other=call):
            return (0, (1 - s[0] if other else s[0]) * half_steps + i)

        out = pl.pallas_call(
            functools.partial(far_kernel, width, call),
            grid_spec=pltpu.PrefetchScalarGridSpec(
                num_scalar_prefetch=1,
                grid=(half_steps,),
                in_specs=[
                    RESIDENT,
                    pl.BlockSpec((count, STEP * width, state_dim), lambda i, s: (0, i, 0)),
                    RESIDENT,
                    RESIDENT,
                    RESIDENT,
                    pl.BlockSpec((1, STEP * width), columns),
                ]
                + [pl.BlockSpec(memory_space=pl.ANY) for _ in before],
                out_specs=pl.BlockSpec((length, STEP * width), columns),
                scratch_shapes=[pltpu.VMEM((STEP, pairs, count * state_dim, 2 * TILE), jnp.bfloat16)],
            ),
            out_shape=shape_of((length, values_dim), jnp.bfloat16),
            input_output_aliases={7: 0} if before else {},
            compiler_params=PARAMS,
            cost_estimate=pl.CostEstimate(flops=10**9, bytes_accessed=6 * 10**6, transcendentals=0),
            name="far",
        )(place, near, states, far_tab, qt, far_factor, gain, *before)
    return out


def solution(mesh):
    return jax.shard_map(
        on_device,
        mesh=mesh,
        in_specs=(
            P(("grp", "seq"), None),
            P(("grp", "seq"), None),
            P(("grp", "seq"), None),
            P(None, ("grp", "seq")),
            P(None, None, ("grp", "seq")),
            P(),
            P(),
        ),
        out_specs=P(("grp", "seq"), None),
        check_vma=False,
    )
```

```python
import functools

import jax
import jax.numpy as jnp
from jax import lax
from jax.experimental import pallas as pl
from jax.experimental.pallas import tpu as pltpu
from jax.sharding import PartitionSpec as P


EPSILON = 1e-05
TILE = 128
GROUP = 16
NEAR_CALLS = (6, 4, 6)
STEP = 2


def log2(value):
    return value.bit_length() - 1


def shape_of(shape, dtype):
    return jax.ShapeDtypeStruct(shape, dtype)


RESIDENT = pl.BlockSpec(memory_space=pltpu.VMEM)
PARAMS = pltpu.CompilerParams(vmem_limit_bytes=24 << 20)


def rows_of(head, width):
    return pl.ds(pl.multiple_of(head * width, width), width)


def tile_decays(log_decay):
    length = log_decay.shape[1]
    row = lax.broadcasted_iota(jnp.int32, (TILE, TILE), 0)
    col = lax.broadcasted_iota(jnp.int32, (TILE, TILE), 1)
    parts = [log_decay[:, at : at + TILE] for at in range(0, length, TILE)]
    local = lax.dot_general(
        jnp.concatenate(parts, axis=0),
        (row <= col).astype(jnp.float32),
        (((1,), (0,)), ((), ())),
        precision=lax.Precision.HIGHEST,
        preferred_element_type=jnp.float32,
    )
    middle = jnp.broadcast_to(local[:, TILE // 2 - 1 : TILE // 2], local.shape)
    total = jnp.broadcast_to(local[:, TILE - 1 : TILE], local.shape)
    heads = log_decay.shape[0]

    def split(array):
        return [array[at : at + heads] for at in range(0, array.shape[0], heads)]

    return split(local), split(middle), split(total)


def pair_row(table, head, pair):
    sides = [table[2 * pair + side, pl.ds(head, 1), :] for side in range(2)]
    return jnp.concatenate(sides, axis=1)


def conv_tile(buf, weight, start):
    taps = weight.shape[0]
    total = None
    for tap in range(taps):
        term = weight[tap : tap + 1, :] * buf[pl.ds(8 - (taps - 1) + tap + start, TILE), :]
        total = term if total is None else total + term
    return total + total * jnp.tanh(total)


def fill(buf, source, rim):
    length = source.shape[0]
    buf[pl.ds(8 - rim.shape[0], rim.shape[0]), :] = rim[...].astype(jnp.float32)
    buf[pl.ds(8, length), :] = source[...].astype(jnp.float32)


def state_keys(pairs):
    return [
        (bit, first)
        for bit in range(log2(pairs))
        for first in range(0, pairs, 2 << bit)
    ]


def three_terms(wide):
    lane = lax.broadcasted_iota(jnp.int32, wide.shape, 1)
    terms = jnp.zeros_like(wide)
    for order in range(3):
        term = wide.astype(jnp.bfloat16).astype(jnp.float32)
        terms = jnp.where(lane == order, term, terms)
        wide = wide - term
    return terms.astype(jnp.bfloat16)


def sum_terms(terms):
    wide = terms.astype(jnp.float32)
    return jnp.broadcast_to(wide[:, 0:1] + wide[:, 1:2] + wide[:, 2:3], wide.shape)


def state_kernel(
    k_ref, v_ref, rim_ref, wk_ref, wv_ref, scale, total, terms_ref, _, _early,
    vt_ref, st_ref, g_ref, kc_ref, values,
    buf, sems,
):
    step = pl.program_id(0)
    heads = scale.shape[1]
    length = v_ref.shape[0]
    width = v_ref.shape[1] // heads
    state_dim = k_ref.shape[1]
    pairs = length // (2 * TILE)
    steps = heads // STEP

    @pl.when(step == 0)
    def _():
        for order in range(steps // 2, steps):
            fetch(v_ref, values, sems, order).start()
        g_ref[pl.ds(heads * width, heads), :] = terms_ref[...]
        fill(buf.at[0], k_ref.at[0:TILE, :], rim_ref.at[:, state_dim : 2 * state_dim])
        kc_ref[0:TILE, :] = conv_tile(buf.at[0], 0.5 * wk_ref[...], 0).astype(jnp.bfloat16)

    for order in range(steps // 2, steps):

        @pl.when(step == order)
        def _(order=order):
            fetch(v_ref, values, sems, order).wait()

    for place in range(STEP):
        lanes = slice(place * width, (place + 1) * width)
        rim_lanes = pl.ds(pl.multiple_of(2 * state_dim + (step * STEP + place) * width, width), width)
        fill(buf.at[place], values.at[step, :, lanes], rim_ref.at[:, rim_lanes])
    for place in range(STEP):
        head = step * STEP + place
        lanes = slice(place * width, (place + 1) * width)
        weight = 0.5 * wv_ref[:, lanes]
        states = {}
        for pair in range(pairs):
            at = 2 * pair * TILE
            sides = []
            for start in (at, at + TILE):
                done = conv_tile(buf.at[place], weight, start).astype(jnp.bfloat16).T
                vt_ref[rows_of(head, width), start : start + TILE] = done
                sides.append(done)
            row = pair_row(scale, head, pair).astype(jnp.bfloat16)
            states[(0, pair)] = jnp.dot(
                jnp.concatenate(sides, axis=1) * row,
                kc_ref[at : at + 2 * TILE, :],
                preferred_element_type=jnp.float32,
            )
        decay = [total[pair, pl.ds(head, 1), :] for pair in range(pairs)]
        for bit in range(log2(pairs)):
            for first in range(0, pairs, 2 << bit):
                keep = states[(bit, first + (1 << bit))]
                factor = decay[first + (1 << bit)]
                for later in range(first + (1 << bit) + 1, first + (2 << bit)):
                    factor = factor * decay[later]
                states[(bit + 1, first)] = keep + factor * states[(bit, first)]
        for order, key in enumerate(state_keys(pairs)):
            st_ref[order, rows_of(head, width), :] = states[key].astype(jnp.bfloat16)
        g_ref[rows_of(head, width), :] = states[(log2(pairs), 0)].astype(jnp.bfloat16)


def table_rows(length):
    inner = log2(GROUP) + 1
    groups = TILE // GROUP
    states = log2(length // (2 * TILE))
    return {
        "inner": 0,
        "group": inner,
        "sibling": inner + groups,
        "value": inner + groups + 1,
        "state": inner + groups + 2,
        "size": inner + groups + 2 + states,
    }


def fetch(v_ref, values, sems, order):
    lanes = slice(order * values.shape[2], (order + 1) * values.shape[2])
    return pltpu.make_async_copy(v_ref.at[:, lanes], values.at[order], sems.at[order])


def table_kernel(
    ld_ref, lw_ref, k_ref, wk_ref, v_ref,
    tab_ref, far_ref, scale_ref, total_ref, terms_ref, kc_ref, values,
    buf, sems,
):
    early = values.shape[0] // 2
    for order in range(early):
        fetch(v_ref, values, sems, order).start()
    heads, length = ld_ref.shape
    levels = lw_ref.shape[0]
    pairs = length // (2 * TILE)
    rows = table_rows(length)
    inner = log2(GROUP) + 1
    tile_level = log2(TILE)
    locals_, middles, totals = tile_decays(ld_ref[...])
    for pair in range(pairs):
        low, high = 2 * pair, 2 * pair + 1
        scale_ref[low] = jnp.exp(totals[low] - locals_[low] + totals[high])
        scale_ref[high] = jnp.exp(totals[high] - locals_[high])
        total_ref[pair] = jnp.exp(totals[low] + totals[high])
    state_dim = k_ref.shape[1]
    weight = 0.5 * wk_ref[:, state_dim : 2 * state_dim]
    buf[pl.ds(8, length), :] = k_ref[...].astype(jnp.float32)
    for at in range(TILE, length, TILE):
        kc_ref[at : at + TILE, :] = conv_tile(buf, weight, at).astype(jnp.bfloat16)
    block = lax.broadcasted_iota(jnp.int32, (heads, TILE), 1) // GROUP
    zero = jnp.zeros((heads, TILE), jnp.float32)
    pair_total = []
    running = zero
    for pair in range(pairs):
        low = 2 * pair
        for tile in (low, low + 1):
            lanes = pl.ds(tile * TILE, TILE)
            weight = [lw_ref[level, :, lanes].astype(jnp.float32) for level in range(levels)]
            local = locals_[tile]
            gap = jnp.exp(local - middles[tile])
            scaled = [weight[level] * gap for level in range(tile_level + 1)]
            for level in range(inner):
                tab_ref[rows["inner"] + level, tile] = scaled[level]
            for group in range(TILE // GROUP):
                base = zero
                differ = block ^ group
                for level in range(inner, tile_level + 1):
                    least = 1 << (level - inner)
                    here = (differ >= least) & (differ < 2 * least) & (block > group)
                    base = jnp.where(here, scaled[level], base)
                tab_ref[rows["group"] + group, tile] = base
            tab_ref[rows["value"], tile] = jnp.exp(middles[tile] - local)
            if tile == low:
                tab_ref[rows["sibling"], tile] = zero
            else:
                tab_ref[rows["sibling"], tile] = weight[tile_level + 1] * jnp.exp(
                    local + totals[low] - middles[low]
                )
                local = local + totals[low]
            for bit in range(log2(pairs)):
                since = zero
                for other in range(pair >> bit << bit, pair):
                    since = since + pair_total[other]
                tab_ref[rows["state"] + bit, tile] = weight[tile_level + 2 + bit] * jnp.exp(
                    local + since
                )
            whole_decay = jnp.exp(local + running)
            first = log2(length) + 1
            for level in range(first, levels):
                far_ref[level - first, tile] = weight[level] * whole_decay
        pair_total.append(totals[low] + totals[low + 1])
        running = running + pair_total[-1]
    terms_ref[...] = three_terms(running)
    for order in range(early):
        fetch(v_ref, values, sems, order).wait()


def rim_kernel(q_ref, k_ref, v_ref, out_ref, last, sems):
    rows, state_dim = out_ref.shape[0], q_ref.shape[1]
    tail = pl.ds(q_ref.shape[0] - GROUP, GROUP)
    lanes = (
        slice(0, state_dim),
        slice(state_dim, 2 * state_dim),
        slice(2 * state_dim, 2 * state_dim + v_ref.shape[1]),
    )
    copies = [
        pltpu.make_async_copy(ref.at[tail, :], last.at[:, at], sems.at[order])
        for order, (ref, at) in enumerate(zip((q_ref, k_ref, v_ref), lanes, strict=True))
    ]
    for copy in copies:
        copy.start()
    for copy in copies:
        copy.wait()
    out_ref[...] = last[GROUP - rows :, :]


def score_kernel(q_ref, rim_ref, w_ref, kc_ref, qt_ref, sc_ref, buf):
    length, state_dim = q_ref.shape
    fill(buf, q_ref, rim_ref.at[:, 0:state_dim])
    weight = 0.5 * w_ref[:, 0:state_dim]
    for at in range(0, length, TILE):
        qt_ref[:, at : at + TILE] = conv_tile(buf, weight, at).astype(jnp.bfloat16).T
    for pair in range(sc_ref.shape[0]):
        at = 2 * pair * TILE
        sc_ref[pair] = jnp.dot(
            kc_ref[at : at + 2 * TILE, :],
            qt_ref[:, at : at + 2 * TILE],
            preferred_element_type=jnp.float32,
        ).astype(jnp.bfloat16)


def near_kernel(first_head, width, vt_ref, st_ref, tab_ref, sc, qt_ref, near_ref, mix, rest):
    length = vt_ref.shape[1]
    pairs = length // (2 * TILE)
    rows = table_rows(length)
    inner = log2(GROUP) + 1
    row = lax.broadcasted_iota(jnp.int32, (GROUP, TILE), 0)
    lane = lax.broadcasted_iota(jnp.int32, (GROUP, TILE), 1)
    within = lane % GROUP
    differ = row ^ within
    keys = state_keys(pairs)

    @pl.when(pl.program_id(0) == 0)
    def _():
        for pair in range(pairs):
            for place in range(STEP):
                mix[place, pair, TILE:, 0:TILE] = jnp.zeros((TILE, TILE), jnp.bfloat16)

    def one_head(place):
        head = first_head + pl.program_id(0) * STEP + place
        own = rows_of(head, width)

        def table(order, tile):
            return tab_ref[order, tile, pl.ds(head, 1), :]

        for pair in range(pairs):
            at = 2 * pair * TILE
            for side in range(2):
                tile = 2 * pair + side
                diagonal = jnp.where(differ == 0, table(rows["inner"], tile), 0.0)
                for level in range(1, inner):
                    here = (differ >= 1 << (level - 1)) & (differ < 1 << level) & (row < within)
                    diagonal = jnp.where(here, table(rows["inner"] + level, tile), diagonal)
                lanes = slice(side * TILE, (side + 1) * TILE)
                for group in range(TILE // GROUP):
                    base = table(rows["group"] + group, tile)
                    weight = jnp.where(lane // GROUP == group, diagonal, base).astype(jnp.bfloat16)
                    start = side * TILE + group * GROUP
                    mix[place, pair, start : start + GROUP, lanes] = (
                        sc[pair, start : start + GROUP, lanes] * weight
                    )
            mix[place, pair, 0:TILE, TILE:] = sc[pair, 0:TILE, TILE:] * table(
                rows["sibling"], 2 * pair + 1
            ).astype(jnp.bfloat16)
            value = vt_ref[own, at : at + 2 * TILE] * pair_row(
                tab_ref.at[rows["value"]], head, pair
            ).astype(jnp.bfloat16)
            summed = jnp.dot(value, mix[place, pair], preferred_element_type=jnp.float32)
            active = [bit for bit in range(log2(pairs)) if pair >> bit & 1]
            if active:
                held = []
                for order, bit in enumerate(active):
                    scale = pair_row(tab_ref.at[rows["state"] + bit], head, pair).astype(jnp.bfloat16)
                    rest[place, pair, order * TILE : (order + 1) * TILE, :] = (
                        qt_ref[:, at : at + 2 * TILE] * scale
                    )
                    held.append(st_ref[keys.index((bit, pair >> bit + 1 << bit + 1)), own, :])
                summed = summed + jnp.dot(
                    jnp.concatenate(held, axis=1),
                    rest[place, pair, 0 : len(active) * TILE, :],
                    preferred_element_type=jnp.float32,
                )
            near_ref[own, at : at + 2 * TILE] = summed.astype(jnp.bfloat16)

    for place in range(STEP):
        one_head(place)


def add_far(levels, head, width, near_ref, buckets, far_ref, qt_ref, off_ref, rest, finish):
    length = qt_ref.shape[1]
    held = jnp.concatenate(buckets, axis=1)
    factors = []
    for level in levels:
        factor = off_ref[level, pl.ds(head, 1), :]
        factors.append(jnp.concatenate([factor, factor], axis=1))
    for pair in range(length // (2 * TILE)):
        at = 2 * pair * TILE
        for order, level in enumerate(levels):
            row = (pair_row(far_ref.at[level], head, pair) * factors[order]).astype(jnp.bfloat16)
            rest[pair, order * TILE : (order + 1) * TILE, :] = qt_ref[:, at : at + 2 * TILE] * row
        summed = near_ref[rows_of(head, width), at : at + 2 * TILE].astype(jnp.float32) + jnp.dot(
            held, rest[pair], preferred_element_type=jnp.float32
        )
        finish(at, summed)


def mid_kernel(
    width, near_ref, chip_ref, low_ref, low_other_ref, far_ref, qt_ref, off_ref, out_ref, rest
):
    step, steps = pl.program_id(0), pl.num_programs(0)
    core, _, _ = position()
    half = steps // 2 * STEP
    for place in range(STEP):
        head = lax.rem(core * (steps // 2) + step, steps) * STEP + place
        rows = rows_of(lax.rem(head, half), width)
        low = jnp.where(step < steps // 2, low_ref[rows, :], low_other_ref[rows, :])

        def finish(at, summed, head=head):
            out_ref[rows_of(head, width), at : at + 2 * TILE] = summed.astype(jnp.bfloat16)

        add_far(
            (0, 1), head, width, near_ref, [chip_ref[rows_of(head, width), :], low], far_ref, qt_ref, off_ref, rest.at[place], finish
        )


def far_kernel(width, other, near_ref, high_ref, far_ref, qt_ref, off_ref, gain_ref, *refs):
    out_ref, rest = refs[-2:]
    count = high_ref.shape[0]
    for place in range(STEP):
        own = slice(place * width, (place + 1) * width)
        core = 1 - position()[0] if other else position()[0]
        head = (core * pl.num_programs(0) + pl.program_id(0)) * STEP + place
        gain = jnp.broadcast_to(gain_ref[:, own], (TILE, TILE)).T

        def finish(at, summed, own=own, gain=gain):
            mean = jnp.mean(summed * summed, axis=0, keepdims=True)
            normed = summed * lax.rsqrt(mean + EPSILON)
            for side in range(2):
                part = normed[:, side * TILE : (side + 1) * TILE] * gain
                start = at + side * TILE
                out_ref[start : start + TILE, own] = part.astype(jnp.bfloat16).T

        add_far(
            tuple(range(2, 2 + count)),
            head,
            width,
            near_ref,
            [high_ref[level, own, :] for level in range(count)],
            far_ref,
            qt_ref,
            off_ref,
            rest.at[place],
            finish,
        )


def position():
    index = lax.axis_index("seq")
    return index & 1, index >> 1 & 1, index >> 2


def core_kernel(width, own_ref, other_ref, theirs_ref, mine_ref, keep_ref, factor):
    heads = keep_ref.shape[1]
    states = heads * width
    quarter = heads // 4
    core, side, _ = position()
    upper = core == 1
    own_total = sum_terms(own_ref[states:, :])
    other_total = sum_terms(other_ref[states:, :])
    factor[...] = jnp.exp(jnp.where(upper, own_total, other_total))
    keep_ref[0] = own_total + other_total
    keep_ref[1] = jnp.where(upper, other_total, 0.0)
    for out_ref, column in ((theirs_ref, 1 - side), (mine_ref, side)):
        for order in range(quarter):
            head = (core * 2 + column) * quarter + order
            own = own_ref[rows_of(head, width), :].astype(jnp.float32)
            other = other_ref[rows_of(head, width), :].astype(jnp.float32)
            scale = factor[pl.ds(head, 1), :]
            last, first = jnp.where(upper, own, other), jnp.where(upper, other, own)
            out_ref[order * width : (order + 1) * width, :] = (last + scale * first).astype(jnp.bfloat16)
    theirs_ref[quarter * width :, :] = three_terms(own_total + other_total)


def side_kernel(width, got_ref, mine_ref, chip_ref, message_ref, keep_ref, factor):
    heads = keep_ref.shape[1]
    quarter = heads // 4
    core, side, _ = position()
    upper = side == 1
    chip_total = chip_ref[0]
    got_total = sum_terms(got_ref[quarter * width :, :])
    factor[...] = jnp.exp(jnp.where(upper, chip_total, got_total))
    keep_ref[0] = chip_ref[1]
    keep_ref[1] = chip_ref[1] + jnp.where(upper, got_total, 0.0)
    for order in range(quarter):
        rows = slice(order * width, (order + 1) * width)
        mine, got = mine_ref[rows, :].astype(jnp.float32), got_ref[rows, :].astype(jnp.float32)
        scale = factor[pl.ds((core * 2 + side) * quarter + order, 1), :]
        last, first = jnp.where(upper, mine, got), jnp.where(upper, got, mine)
        message_ref[rows, :] = (last + scale * first).astype(jnp.bfloat16)
    message_ref[quarter * width :, :] = three_terms(chip_total + got_total)


def plane_kernel(width, *refs):
    far_ref, part_ref, factor = refs[-3:]
    came, keep_ref = refs[:-4], refs[-4]
    heads = keep_ref.shape[1]
    quarter = heads // 4
    core, side, plane = position()
    planes = len(came) + 1
    totals = [sum_terms(ref[quarter * width :, :]) for ref in came]
    zero = jnp.zeros_like(totals[0])
    far_ref[0] = jnp.where(core == 1, jnp.ones_like(zero), 0.0)
    far_ref[1] = jnp.where(side == 1, jnp.exp(keep_ref[0]), 0.0)
    in_plane = jnp.exp(keep_ref[1])
    for bit in range(log2(planes)):
        upper = (plane >> bit) & 1 == 1
        far_ref[2 + bit] = jnp.where(upper, in_plane, 0.0)
        if bit == 0:
            continue
        for by in range(1, planes):
            source = plane ^ by
            here = upper & (source >> (bit + 1) == plane >> (bit + 1)) & ((source >> bit) & 1 == 0)
            between = zero
            for mid in range(1, planes):
                inside = (plane ^ mid > source) & (plane ^ mid < plane)
                between = between + jnp.where(inside, totals[mid - 1], 0.0)
            factor[by - 1] = jnp.where(here, jnp.exp(between), 0.0)
        for order in range(quarter):
            rows = slice(order * width, (order + 1) * width)
            head = (core * 2 + side) * quarter + order
            summed = None
            for by in range(1, planes):
                term = factor[by - 1, pl.ds(head, 1), :] * came[by - 1][rows, :].astype(jnp.float32)
                summed = term if summed is None else summed + term
            part_ref[bit - 1, rows, :] = summed.astype(jnp.bfloat16)


def stack_kernel(first_ref, last_ref, out_ref):
    half = first_ref.shape[0]
    out_ref[0:half, :] = first_ref[...]
    out_ref[half:, :] = last_ref[0:half, :]


def column_kernel(next_ref, next_swapped_ref, part_ref, swapped_ref, out_ref):
    _, side, _ = position()
    count, quarter, _ = part_ref.shape
    mine, theirs = rows_of(side, quarter), rows_of(1 - side, quarter)
    out_ref[0, mine, :] = next_ref[0:quarter, :]
    out_ref[0, theirs, :] = next_swapped_ref[0:quarter, :]
    for level in range(count):
        out_ref[level + 1, mine, :] = part_ref[level]
        out_ref[level + 1, theirs, :] = swapped_ref[level]


def glue(kernel, out_shape, scratch=()):
    def call(*args):
        many = isinstance(out_shape, list)
        return pl.pallas_call(
            kernel,
            in_specs=[RESIDENT for _ in args],
            out_specs=[RESIDENT for _ in out_shape] if many else RESIDENT,
            out_shape=out_shape,
            scratch_shapes=list(scratch),
            compiler_params=PARAMS,
            cost_estimate=pl.CostEstimate(flops=10**7, bytes_accessed=10**6, transcendentals=0),
        )(*args)

    return call


def send(x, by, size):
    return lax.ppermute(x, "seq", [(i, i ^ by) for i in range(size)])


def on_device(
    query_inputs, key_inputs, value_inputs, log_decay, level_weight, conv_weight, norm_gain
):
    length, state_dim = query_inputs.shape
    heads = log_decay.shape[0]
    values_dim = value_inputs.shape[1]
    width = values_dim // heads
    taps = conv_weight.shape[0]
    rim = taps - 1
    size = lax.axis_size("seq")
    bits = log2(size)
    pairs = length // (2 * TILE)
    keys = state_keys(pairs)
    half, quarter = values_dim // 2, values_dim // 4
    half_heads = heads // 2
    tail = heads
    half_steps = half_heads // STEP
    gain = norm_gain.reshape(1, values_dim)
    planes = size // 4
    rows = table_rows(length)
    value_inputs = pltpu.with_memory_space_constraint(value_inputs, pltpu.HBM)
    calls = NEAR_CALLS if sum(NEAR_CALLS) == heads else (heads,)

    rim_width = 2 * state_dim + values_dim
    own_rim = pl.pallas_call(
        rim_kernel,
        in_specs=[pl.BlockSpec(memory_space=pltpu.HBM)] * 3,
        out_specs=RESIDENT,
        out_shape=pltpu.VMEM((rim, rim_width), jnp.bfloat16),
        scratch_shapes=[
            pltpu.VMEM((GROUP, rim_width), jnp.bfloat16),
            pltpu.SemaphoreType.DMA((3,)),
        ],
        compiler_params=pltpu.CompilerParams(vmem_limit_bytes=62 << 20),
        name="rim",
    )(query_inputs, key_inputs, value_inputs)
    rims = lax.ppermute(own_rim, "seq", [(i, i + 1) for i in range(size - 1)])

    tab, far_tab, scale, total, terms, kc, values = pl.pallas_call(
        table_kernel,
        in_specs=[RESIDENT] * 4 + [pl.BlockSpec(memory_space=pl.ANY)],
        out_specs=[RESIDENT] * 7,
        out_shape=[
            pltpu.VMEM((rows["size"], length // TILE, heads, TILE), jnp.float32),
            pltpu.VMEM((bits, length // TILE, heads, TILE), jnp.float32),
            pltpu.VMEM((length // TILE, heads, TILE), jnp.float32),
            pltpu.VMEM((pairs, heads, TILE), jnp.float32),
            pltpu.VMEM((heads, TILE), jnp.bfloat16),
            pltpu.VMEM((length, state_dim), jnp.bfloat16),
            pltpu.VMEM((heads // STEP, length, STEP * width), jnp.bfloat16),
        ],
        scratch_shapes=[
            pltpu.VMEM((length + 8, TILE), jnp.float32),
            pltpu.SemaphoreType.DMA((heads // STEP,)),
        ],
        compiler_params=PARAMS,
        cost_estimate=pl.CostEstimate(flops=10**9, bytes_accessed=3 * 10**6, transcendentals=0),
        name="tables",
    )(log_decay, level_weight, key_inputs, conv_weight, value_inputs)

    vt, st, group, kc, _ = pl.pallas_call(
        state_kernel,
        grid=(heads // STEP,),
        in_specs=[
            RESIDENT,
            pl.BlockSpec(memory_space=pl.ANY),
            RESIDENT,
            pl.BlockSpec((taps, state_dim), lambda i: (0, 1)),
            pl.BlockSpec((taps, STEP * width), lambda i: (0, 2 * state_dim // (STEP * width) + i)),
            RESIDENT,
            RESIDENT,
            RESIDENT,
            RESIDENT,
            RESIDENT,
        ],
        input_output_aliases={8: 3, 9: 4},
        out_specs=[RESIDENT] * 5,
        out_shape=[
            pltpu.VMEM((values_dim, length), jnp.bfloat16),
            pltpu.VMEM((len(keys), values_dim, state_dim), jnp.bfloat16),
            pltpu.VMEM((values_dim + tail, state_dim), jnp.bfloat16),
            pltpu.VMEM((length, state_dim), jnp.bfloat16),
            pltpu.VMEM((heads // STEP, length, STEP * width), jnp.bfloat16),
        ],
        scratch_shapes=[
            pltpu.VMEM((STEP, length + 8, TILE), jnp.float32),
            pltpu.SemaphoreType.DMA((heads // STEP,)),
        ],
        compiler_params=PARAMS,
        cost_estimate=pl.CostEstimate(flops=10**9, bytes_accessed=9 * 10**6, transcendentals=0),
        name="state",
    )(key_inputs, value_inputs, rims, conv_weight, conv_weight, scale, total, terms, kc, values)

    qt, sc = pl.pallas_call(
        score_kernel,
        in_specs=[RESIDENT] * 4,
        out_specs=[RESIDENT] * 2,
        out_shape=[
            pltpu.VMEM((state_dim, length), jnp.bfloat16),
            pltpu.VMEM((pairs, 2 * TILE, 2 * TILE), jnp.bfloat16),
        ],
        scratch_shapes=[pltpu.VMEM((length + 8, TILE), jnp.float32)],
        compiler_params=PARAMS,
        cost_estimate=pl.CostEstimate(flops=10**8, bytes_accessed=10**6, transcendentals=0),
        name="scores",
    )(query_inputs, rims, conv_weight, kc)

    near = vt
    for call, each in enumerate(calls):
        near = pl.pallas_call(
            functools.partial(near_kernel, sum(calls[:call]), width),
            grid=(each // STEP,),
            in_specs=[RESIDENT] * 5,
            out_specs=RESIDENT,
            out_shape=pltpu.VMEM((values_dim, length), jnp.bfloat16),
            scratch_shapes=[
                pltpu.VMEM((STEP, pairs, 2 * TILE, 2 * TILE), jnp.bfloat16),
                pltpu.VMEM((STEP, pairs, log2(pairs) * state_dim, 2 * TILE), jnp.bfloat16),
            ],
            input_output_aliases={0: 0},
            compiler_params=PARAMS,
            cost_estimate=pl.CostEstimate(flops=10**9, bytes_accessed=4 * 10**6, transcendentals=0),
            name="near",
        )(near, st, tab, sc, qt)

    other = send(group, 1, size)
    table = pltpu.VMEM((heads, state_dim), jnp.float32)
    message_shape = pltpu.VMEM((quarter + tail, state_dim), jnp.bfloat16)
    theirs, mine, keep = glue(
        functools.partial(core_kernel, width),
        [
            message_shape,
            pltpu.VMEM((quarter, state_dim), jnp.bfloat16),
            pltpu.VMEM((2, heads, state_dim), jnp.float32),
        ],
        [table],
    )(group, other)

    got = send(theirs, 2, size)
    got_rest = send(mine, 2, size)
    message, keep = glue(
        functools.partial(side_kernel, width),
        [message_shape, pltpu.VMEM((2, heads, state_dim), jnp.float32)],
        [table],
    )(got, mine, keep)

    came = []
    for by in range(1, planes):
        came.append(send(message, 4 * by, size))

    next_swapped = send(came[0], 2, size)

    low = glue(stack_kernel, pltpu.VMEM((half, state_dim), jnp.bfloat16))(got_rest, got)
    low_other = send(low, 1, size)

    count = bits - 2
    far_factor, part = glue(
        functools.partial(plane_kernel, width),
        [
            pltpu.VMEM((bits, heads, state_dim), jnp.float32),
            pltpu.VMEM((count - 1, quarter, state_dim), jnp.bfloat16),
        ],
        [pltpu.VMEM((planes - 1, heads, state_dim), jnp.float32)],
    )(*came, keep)

    near = pl.pallas_call(
        functools.partial(mid_kernel, width),
        grid=(2 * half_steps,),
        in_specs=[RESIDENT] * 7,
        out_specs=RESIDENT,
        scratch_shapes=[pltpu.VMEM((STEP, pairs, 2 * state_dim, 2 * TILE), jnp.bfloat16)],
        out_shape=pltpu.VMEM((values_dim, length), jnp.bfloat16),
        input_output_aliases={0: 0},
        compiler_params=PARAMS,
        cost_estimate=pl.CostEstimate(flops=10**9, bytes_accessed=6 * 10**6, transcendentals=0),
        name="mid",
    )(near, other, low, low_other, far_tab, qt, far_factor)

    swapped = send(part, 2, size)
    high = glue(column_kernel, pltpu.VMEM((count, half, state_dim), jnp.bfloat16))(
        came[0], next_swapped, part, swapped
    )
    high_other = send(high, 1, size)

    out = None
    for call, states in enumerate((high, high_other)):
        before = [] if out is None else [out]

        def columns(i, other=call):
            core = position()[0]
            return (0, (1 - core if other else core) * half_steps + i)

        out = pl.pallas_call(
            functools.partial(far_kernel, width, call),
            grid=(half_steps,),
            in_specs=[
                RESIDENT,
                pl.BlockSpec((count, STEP * width, state_dim), lambda i: (0, i, 0)),
                RESIDENT,
                RESIDENT,
                RESIDENT,
                pl.BlockSpec((1, STEP * width), columns),
            ]
            + [pl.BlockSpec(memory_space=pl.ANY) for _ in before],
            out_specs=pl.BlockSpec((length, STEP * width), columns),
            scratch_shapes=[pltpu.VMEM((STEP, pairs, count * state_dim, 2 * TILE), jnp.bfloat16)],
            out_shape=shape_of((length, values_dim), jnp.bfloat16),
            input_output_aliases={6: 0} if before else {},
            compiler_params=PARAMS,
            cost_estimate=pl.CostEstimate(flops=10**9, bytes_accessed=6 * 10**6, transcendentals=0),
            name="far",
        )(near, states, far_tab, qt, far_factor, gain, *before)
    return out


def solution(mesh):
    return jax.shard_map(
        on_device,
        mesh=mesh,
        in_specs=(
            P(("grp", "seq"), None),
            P(("grp", "seq"), None),
            P(("grp", "seq"), None),
            P(None, ("grp", "seq")),
            P(None, None, ("grp", "seq")),
            P(),
            P(),
        ),
        out_specs=P(("grp", "seq"), None),
        check_vma=False,
    )
```
